128 devices in a mesh: ctx: 32 (over x, y, core), head: 4 (over z).
Axes of the slice: x: 4, y: 4, z: 4, core: 2. Of those that a mesh axis runs over, the one named last changes fastest.
Arguments:
- queries: bfloat16 [2, 8192, 16384], P(None, 'ctx', 'head'), may hold values from -900 to 900
- key_input: bfloat16 [2, 8192, 1024], P(None, 'ctx', 'head'), may hold values from -900 to 900
- values: bfloat16 [2, 8192, 1024], P(None, 'ctx', 'head'), may hold values from -40 to 40
- query_map: bfloat16 [128, 128, 128], P('head'), may hold values from -0.5 to 0.5
- key_map: bfloat16 [8, 128, 128], P('head'), may hold values from -0.5 to 0.5
- out_gain: bfloat16 [16384], P('head'), may hold values from 0.099609375 to 1.8984375
- rank_in: bfloat16 [16384, 512], P('head'), may hold values from -0.046875 to 0.046875
- rank_out: bfloat16 [512, 16384], P(None, 'head'), may hold values from -0.25 to 0.25
Outputs:
- layer_out: bfloat16 [2, 8192, 16384], P(None, 'ctx', 'head')
The draws below stay inside these ranges and needn't reach their ends.
All inputs are finite; a program needn't handle non-finite values.
Results may differ from the reference program's by a relative error of at most 0.006.
Values may be sent and summed in bfloat16 or wider, within the bound.
A program may use at most 128 MiB of HBM per device.

```python
import math
import jax
import jax.numpy as jnp
from jax import lax

D = 16384
H = 128
KVH = 8
HD = 128
FEAT = 128
RANK = 512
BLK = 256
SEQS = 2
CTXLEN = 8192


def spiky_draw(key, full_shape):
    key_base = jax.random.fold_in(key, 0)
    drawn = jnp.clip(jax.random.normal(key_base, full_shape, jnp.float32), -6.0, 6.0)
    return drawn


def draw_queries(key, part):
    return spiky_draw(jax.random.fold_in(key, 11), (SEQS, CTXLEN, H * HD)).astype(jnp.bfloat16)


def draw_key_input(key, part):
    return spiky_draw(jax.random.fold_in(key, 12), (SEQS, CTXLEN, KVH * HD)).astype(jnp.bfloat16)


def draw_values(key, part):
    key_base, key_column = jax.random.split(jax.random.fold_in(key, 13), 2)
    full_shape = (SEQS, CTXLEN, KVH * HD)
    column = (jnp.arange(KVH * HD) // HD).astype(jnp.float32)
    rising = jnp.exp(math.log(3.0) * column / max(KVH - 1, 1))
    spread = jnp.exp(jax.random.uniform(key_column, (KVH * HD,), jnp.float32, math.log(0.5), math.log(2.0)))
    drawn = jnp.clip(jax.random.normal(key_base, full_shape, jnp.float32), -6.0, 6.0)
    return (drawn * rising * spread).astype(jnp.bfloat16)


def block_levels(stream_key, extent, cuts, least, high):
    def one(dim, parts):
        heights = jax.random.uniform(jax.random.fold_in(jax.random.fold_in(stream_key, 6), dim), (parts,), jnp.float32, least / len(cuts), high / len(cuts))
        return jnp.repeat(jnp.exp(heights), extent[dim] // parts).reshape((-1,) + (1,) * (len(extent) - dim - 1))

    level = one(*cuts[0])
    for cut in cuts[1:]:
        level = level * one(*cut)
    return level


def bell_draw(stream_key, dims, scale, limit, cuts=(), kind=jnp.bfloat16):
    entries = scale * jax.random.normal(stream_key, dims, jnp.float32)
    if cuts:
        entries = entries * block_levels(stream_key, dims, cuts, -0.22, 0.18)
    return jnp.clip(entries, -limit, limit).astype(kind)


def setup_inputs(seed: int = 0) -> dict:
    arg_keys = jax.random.split(jax.random.key(seed), 9)
    queries = draw_queries(jax.random.fold_in(arg_keys[8], 71), 0)
    key_input = draw_key_input(jax.random.fold_in(arg_keys[8], 71), 0)
    values = draw_values(jax.random.fold_in(arg_keys[8], 71), 0)
    query_map = bell_draw(arg_keys[3], (H, HD, FEAT), HD ** -0.5, 0.5, ((0, 4),))
    key_map = bell_draw(arg_keys[4], (KVH, HD, FEAT), HD ** -0.5, 0.5, ((0, 4),))
    out_gain = jnp.clip(1.0 + 0.18 * jax.random.normal(arg_keys[5], (H * HD,), jnp.float32), 0.099609375, 1.8984375).astype(jnp.bfloat16)
    rank_in = bell_draw(arg_keys[6], (H * HD, RANK), (H * HD) ** -0.5, 0.046875, ((0, 4),))
    rank_out = bell_draw(arg_keys[7], (RANK, D), RANK ** -0.5, 0.25, ((1, 4),))
    return {"queries": queries, "key_input": key_input, "values": values, "query_map": query_map, "key_map": key_map, "out_gain": out_gain, "rank_in": rank_in, "rank_out": rank_out}


def rounded(inputs):
    return lax.optimization_barrier(inputs.astype(jnp.bfloat16)).astype(jnp.float32)

def feature_pair(inputs, weight, form):
    scores = jnp.einsum(form, inputs.astype(jnp.float32), weight.astype(jnp.float32))
    joined = jnp.concatenate([jax.nn.softmax(scores, axis=-1), jax.nn.softmax(-scores, axis=-1)], axis=-1)
    return rounded(joined)

def exclusive_sum(inputs):
    running = jnp.cumsum(inputs, axis=1)
    return jnp.concatenate([jnp.zeros_like(inputs[:, :1]), running[:, :-1]], axis=1)

def group_attention(operands):
    query_group, key_group, value_group, qmap_group, kmap_group = operands
    seqs_here = query_group.shape[0]
    blocks = query_group.shape[1] // BLK
    groups = query_group.shape[2]
    feat_query = feature_pair(query_group, qmap_group, 'sngd,gdf->sngf')
    feat_key = feature_pair(key_group, kmap_group, 'snd,df->snf')
    fq_blocks = feat_query.reshape(seqs_here, blocks, BLK, groups, 2 * FEAT)
    fk_blocks = feat_key.reshape(seqs_here, blocks, BLK, 2 * FEAT)
    v_blocks = value_group.astype(jnp.float32).reshape(seqs_here, blocks, BLK, HD)
    states = jnp.einsum('sbtf,sbtd->sbfd', fk_blocks, v_blocks)
    key_sums = lax.optimization_barrier(jnp.sum(fk_blocks, axis=2))
    prefix = rounded(exclusive_sum(states))
    prefix_sum = rounded(exclusive_sum(key_sums))
    scores = jnp.einsum('sbtqf,sbuf->sbqtu', fq_blocks, fk_blocks)
    causal = jnp.arange(BLK)[:, None] >= jnp.arange(BLK)[None, :]
    scores = jnp.where(causal, scores, jnp.float32(0.0))
    local_den = jnp.swapaxes(lax.optimization_barrier(jnp.sum(scores, axis=-1)), 2, 3)
    weights = rounded(scores)
    local_num = jnp.einsum('sbqtu,sbud->sbtqd', weights, v_blocks)
    carried_num = jnp.einsum('sbtqf,sbfd->sbtqd', fq_blocks, prefix)
    carried_den = jnp.einsum('sbtqf,sbf->sbtq', fq_blocks, prefix_sum)
    mixed = (local_num + carried_num) / (local_den + carried_den)[..., None]
    return mixed.reshape(seqs_here, blocks * BLK, groups * HD)

def reference(queries, key_input, values, query_map, key_map, out_gain, rank_in, rank_out):
    seqs_here = queries.shape[0]
    length = queries.shape[1]
    groups = H // KVH
    query_stack = jnp.moveaxis(queries.reshape(seqs_here, length, KVH, groups, HD), 2, 0)
    key_stack = jnp.moveaxis(key_input.reshape(seqs_here, length, KVH, HD), 2, 0)
    value_stack = jnp.moveaxis(values.reshape(seqs_here, length, KVH, HD), 2, 0)
    qmap_stack = query_map.reshape(KVH, groups, HD, FEAT)
    attended = lax.map(group_attention, (query_stack, key_stack, value_stack, qmap_stack, key_map))
    attended = jnp.moveaxis(attended, 0, 2).reshape(seqs_here * length, H * HD)
    mean_square = lax.optimization_barrier(jnp.sum(attended * attended, axis=-1, keepdims=True)) / (H * HD)
    normed = (attended * lax.rsqrt(mean_square + 1e-05) * out_gain.astype(jnp.float32)).astype(jnp.bfloat16)
    reduced = jnp.dot(normed, rank_in, preferred_element_type=jnp.float32).astype(jnp.bfloat16)
    result = jnp.dot(reduced, rank_out, preferred_element_type=jnp.float32).astype(jnp.bfloat16)
    return result.reshape(seqs_here, length, D)
```

```python
import functools

import jax
import jax.numpy as jnp
from jax import lax
from jax.experimental import pallas as pl
from jax.experimental.pallas import tpu as pltpu
from jax.sharding import PartitionSpec as P

HD = 128
BLK = 256
SEQS = 2
LOG2E = 1.4426950408889634
MESH = pl.DeviceIdType.MESH
bf16, f32 = jnp.bfloat16, jnp.float32


def nn(a, b):
    return jnp.dot(a, b, preferred_element_type=f32)


def tt(a, b):
    return lax.dot_general(a, b, (((0,), (1,)), ((), ())), preferred_element_type=f32)


def exps(scores):
    scaled = scores * LOG2E
    pos = jnp.exp2(scaled - jnp.max(scaled, axis=0, keepdims=True))
    neg = jnp.exp2(jnp.min(scaled, axis=0, keepdims=True) - scaled)
    return pos, neg, jnp.sum(pos, axis=0, keepdims=True), jnp.sum(neg, axis=0, keepdims=True)


def kernel(nc, nz, feats, q_hbm, k_hbm, v_hbm, qm_hbm, km_hbm, gain_ref, ri_hbm, out_ref,
           q_v, k_v, v_v, qm_v, km_v, ri_v, rit, gcol, fk, vta, pta, fq, wb, att, ssq, part,
           send_e, recv_e, send_p, recv_p, msg, got, red,
           in_sem, s1, r1, s2, r2, s3, r3, s4, r4):
    hl, kvl = qm_v.shape[0], km_v.shape[0]
    groups = hl // kvl
    rank = ri_v.shape[1]
    rb = rank // nz
    rows = send_e.shape[1]
    per = HD // rows
    mc, mz = lax.axis_index("ctx"), lax.axis_index("head")

    loads = [(k_hbm, k_v), (v_hbm, v_v), (km_hbm, km_v), (qm_hbm, qm_v),
             (q_hbm.at[0], q_v.at[0]), (ri_hbm, ri_v), (q_hbm.at[1], q_v.at[1])]
    loads = [pltpu.make_async_copy(a, b, in_sem.at[i]) for i, (a, b) in enumerate(loads)]
    for load in loads:
        load.start()

    barrier = pltpu.get_barrier_semaphore()

    def greet_ctx(i, _):
        pl.semaphore_signal(barrier, inc=1, device_id=(lax.rem(mc + i, nc), mz), device_id_type=MESH)
        return 0

    lax.fori_loop(1, nc, greet_ctx, 0)
    for i in range(1, nz):
        pl.semaphore_signal(barrier, inc=1, device_id=(mc, lax.rem(mz + i, nz)), device_id_type=MESH)

    for load in loads[:3]:
        load.wait()
    first = lax.broadcasted_iota(jnp.int32, (rows, HD), 0) == 0
    for s in range(SEQS):
        for g in range(kvl):
            i = s * kvl + g
            lanes = slice(g * HD, (g + 1) * HD)
            pos, neg, zp, zn = exps(tt(km_v[g], k_v[s, :, lanes]))
            feat = jnp.concatenate([pos * (1.0 / zp), neg * (1.0 / zn)], axis=0).astype(bf16)
            fk[i] = feat.T
            vta[i, 0:HD, :] = v_v[s, :, lanes].T
            vta[i, HD:HD + 16, :] = jnp.ones((16, BLK), bf16)
            state = nn(vta[i], fk[i])
            for p in range(per):
                j = i * per + p
                send_e[j, :, 0:2 * HD] = state[p * rows:(p + 1) * rows].astype(bf16)
                send_e[j, :, 2 * HD:] = jnp.where(
                    first, state[HD:HD + 1, 0:HD], state[HD:HD + 1, HD:2 * HD]).astype(bf16)

    pl.semaphore_wait(barrier, nc - 1 + nz - 1)

    def exchange(src, dst, ssem, rsem, i):
        to = lax.rem(mc + i, nc)
        return pltpu.make_async_remote_copy(
            src_ref=src.at[to], dst_ref=dst.at[mc], send_sem=ssem.at[i], recv_sem=rsem.at[i],
            device_id=(to, mz), device_id_type=MESH)

    def arrival(src, dst, ssem, rsem, i):
        at = lax.rem(mc + nc - i, nc)
        return pltpu.make_async_remote_copy(
            src_ref=src.at[at], dst_ref=dst.at[at], send_sem=ssem.at[i], recv_sem=rsem.at[i],
            device_id=(at, mz), device_id_type=MESH)

    def start1(i, _):
        exchange(send_e, recv_e, s1, r1, i).start()
        return 0

    lax.fori_loop(1, nc, start1, 0)
    recv_e[mc] = send_e[mc]

    for load in loads[3:6]:
        load.wait()

    upper = (lax.broadcasted_iota(jnp.int32, (BLK, BLK), 0)
             <= lax.broadcasted_iota(jnp.int32, (BLK, BLK), 1))

    def features(s, h):
        g = s * kvl + h // groups
        pos, neg, zp, zn = exps(tt(qm_v[h], q_v[s, :, pl.ds(pl.multiple_of(h * HD, HD), HD)]))
        feat = jnp.concatenate([pos, neg * (zp / zn)], axis=0).astype(bf16)
        fq[s * hl + h] = feat
        wb[s * hl + h] = jnp.where(upper, nn(fk[g], feat), 0.0).astype(bf16)

    def prepare(h):
        gain = gain_ref[0:1, pl.ds(pl.multiple_of(h * HD, HD), HD)].astype(f32)
        gcol[h] = jnp.broadcast_to(gain, (HD, HD)).T
        rit[:, pl.ds(pl.multiple_of(h * HD, HD), HD)] = ri_v[pl.ds(pl.multiple_of(h * HD, HD), HD), :].T

    def attend(s, h):
        g = s * kvl + h // groups
        total = nn(vta[g], wb[s * hl + h]) + nn(pta[g], fq[s * hl + h])
        out = total[0:HD] * (1.0 / total[HD:HD + 1])
        ssq[s] += jnp.sum((out * out).reshape(HD // 16, 16, BLK), axis=0)
        scale = gcol[h]
        att[s, pl.ds(pl.multiple_of(h * HD, HD), HD), :] = jnp.concatenate(
            [out[:, 0:HD] * scale, out[:, HD:] * scale], axis=1).astype(bf16)

    def loop(start, stop, step, body):
        def trip(i, _):
            for j in range(step):
                body(start + i * step + j)
            return 0
        lax.fori_loop(0, (stop - start) // step, trip, 0)

    def body0(h):
        features(0, h)
        prepare(h)

    loop(0, hl, 2, body0)
    loads[6].wait()

    def wait1(i, _):
        arrival(send_e, recv_e, s1, r1, i).wait_recv()
        return 0

    lax.fori_loop(1, nc, wait1, 0)

    def scan(i, total):
        send_p[i] = total.astype(bf16)
        return total + recv_e[i].astype(f32)

    lax.fori_loop(0, nc, scan, jnp.zeros(send_p.shape[1:], f32))

    def start2(i, _):
        exchange(send_p, recv_p, s2, r2, i).start()
        return 0

    lax.fori_loop(1, nc, start2, 0)
    recv_p[mc] = send_p[mc]

    loop(0, hl, 2, lambda h: features(1, h))

    def wait2(i, _):
        arrival(send_p, recv_p, s2, r2, i).wait_recv()
        return 0

    lax.fori_loop(1, nc, wait2, 0)
    for i in range(SEQS * kvl):
        for p in range(per):
            pta[i, p * rows:(p + 1) * rows, :] = recv_p[i * per + p, :, 0:2 * HD]
        sums = recv_p[i * per, 0:2, 2 * HD:].astype(f32)
        pta[i, HD:HD + 16, :] = jnp.broadcast_to(
            jnp.concatenate([sums[0:1], sums[1:2]], axis=1), (16, BLK)).astype(bf16)

    ssq[...] = jnp.zeros_like(ssq)

    def partner(s, i):
        return lax.rem(mz + i, nz)

    def scatter(s, i):
        to = lax.rem(mz + i, nz)
        return pltpu.make_async_remote_copy(
            src_ref=msg.at[s, to], dst_ref=got.at[s, i - 1], send_sem=s3.at[s, i], recv_sem=r3.at[s, i],
            device_id=(mc, to), device_id_type=MESH)

    def gather(s, i, at):
        to = lax.rem(mz + i, nz)
        return pltpu.make_async_remote_copy(
            src_ref=red.at[s, at], dst_ref=red.at[s, at], send_sem=s4.at[s, i], recv_sem=r4.at[s, i],
            device_id=(mc, to), device_id_type=MESH)

    def project(s):
        part[s] = nn(rit[...], att[s])
        for p in range(nz):
            msg[s, p, 0:rb, :] = part[s, p * rb:(p + 1) * rb, :].astype(bf16)
            msg[s, p, rb:, :] = ssq[s].astype(bf16)
        for i in range(1, nz):
            scatter(s, i).start()

    def reduce(s):
        for i in range(1, nz):
            scatter(s, i).wait_recv()
        total = part[s, pl.ds(pl.multiple_of(mz * rb, rb), rb), :]
        squares = ssq[s]
        for i in range(1, nz):
            total = total + got[s, i - 1, 0:rb, :].astype(f32)
            squares = squares + got[s, i - 1, rb:, :].astype(f32)
        factor = lax.rsqrt(jnp.sum(squares, axis=0, keepdims=True) / feats + 1e-05)
        red[s, mz] = (total * factor).astype(bf16)
        for i in range(1, nz):
            gather(s, i, mz).start()

    loop(0, hl, 2, lambda h: attend(0, h))
    project(0)
    loop(0, hl // 2, 2, lambda h: attend(1, h))
    reduce(0)
    loop(hl // 2, hl, 2, lambda h: attend(1, h))
    project(1)
    reduce(1)
    for s in range(SEQS):
        for i in range(1, nz):
            gather(s, i, lax.rem(mz + nz - i, nz)).wait_recv()
        for p in range(nz):
            out_ref[s, p * rb:(p + 1) * rb, :] = red[s, p]

    def drain(i, _):
        exchange(send_e, recv_e, s1, r1, i).wait_send()
        exchange(send_p, recv_p, s2, r2, i).wait_send()
        return 0

    lax.fori_loop(1, nc, drain, 0)
    for s in range(SEQS):
        for i in range(1, nz):
            scatter(s, i).wait_send()
            gather(s, i, mz).wait_send()


def attention(nc, nz, q, k, v, qm, km, gain, ri):
    hl, kvl, rank = qm.shape[0], km.shape[0], ri.shape[1]
    rows = SEQS * kvl * HD // nc
    rb = rank // nz
    states = SEQS * kvl
    vm, dma = pltpu.VMEM, pltpu.SemaphoreType.DMA
    hbm = pl.BlockSpec(memory_space=pl.ANY)
    vmem = pl.BlockSpec(memory_space=pltpu.VMEM)
    return pl.pallas_call(
        functools.partial(kernel, nc, nz, float(nz * hl * HD)),
        out_shape=jax.ShapeDtypeStruct((SEQS, rank, BLK), bf16),
        in_specs=[hbm, hbm, hbm, hbm, hbm, vmem, hbm],
        out_specs=vmem,
        scratch_shapes=[
            vm(q.shape, bf16), vm(k.shape, bf16), vm(v.shape, bf16), vm(qm.shape, bf16),
            vm(km.shape, bf16), vm(ri.shape, bf16), vm((rank, hl * HD), bf16), vm((hl, HD, HD), f32),
            vm((states, BLK, 2 * HD), bf16), vm((states, HD + 16, BLK), bf16), vm((states, HD + 16, 2 * HD), bf16),
            vm((SEQS * hl, 2 * HD, BLK), bf16), vm((SEQS * hl, BLK, BLK), bf16),
            vm((SEQS, hl * HD, BLK), bf16), vm((SEQS, 16, BLK), f32), vm((SEQS, rank, BLK), f32),
            vm((nc, rows, 3 * HD), bf16), vm((nc, rows, 3 * HD), bf16),
            vm((nc, rows, 3 * HD), bf16), vm((nc, rows, 3 * HD), bf16),
            vm((SEQS, nz, rb + 16, BLK), bf16), vm((SEQS, nz - 1, rb + 16, BLK), bf16),
            vm((SEQS, nz, rb, BLK), bf16),
            dma((7,)), dma((nc,)), dma((nc,)), dma((nc,)), dma((nc,)),
            dma((SEQS, nz)), dma((SEQS, nz)), dma((SEQS, nz)), dma((SEQS, nz)),
        ],
        compiler_params=pltpu.CompilerParams(
            collective_id=0, has_side_effects=True, vmem_limit_bytes=60 * 2**20),
        name="attention",
    )(q, k, v, qm, km, gain, ri)


def solution(mesh):
    nc, nz = mesh.shape["ctx"], mesh.shape["head"]

    def shards(queries, key_input, values, query_map, key_map, out_gain, rank_in, rank_out):
        reduced = attention(nc, nz, queries, key_input, values, query_map, key_map,
                            out_gain.reshape(1, -1), rank_in)
        result = lax.dot_general(reduced, rank_out, (((1,), (0,)), ((), ())), preferred_element_type=f32)
        return result.astype(bf16)

    in_specs = (
        P(None, "ctx", "head"),
        P(None, "ctx", "head"),
        P(None, "ctx", "head"),
        P("head", None, None),
        P("head", None, None),
        P("head"),
        P("head", None),
        P(None, "head"),
    )
    out_specs = P(None, "ctx", "head")
    return jax.shard_map(shards, mesh=mesh, in_specs=in_specs, out_specs=out_specs, check_vma=False)
```

```python
import functools

import jax
import jax.numpy as jnp
from jax import lax
from jax.experimental import pallas as pl
from jax.experimental.pallas import tpu as pltpu
from jax.sharding import PartitionSpec as P

HD = 128
BLK = 256
SEQS = 2
ST, AT = 8, 8
VLIM = 59
LOG2E = 1.4426950408889634
MESH = pl.DeviceIdType.MESH
bf16, f32 = jnp.bfloat16, jnp.float32


def nn(a, b):
    return jnp.dot(a, b, preferred_element_type=f32)


def tt(a, b):
    return lax.dot_general(a, b, (((0,), (1,)), ((), ())), preferred_element_type=f32)


def exps(scaled):
    pos = jnp.exp2(scaled - jnp.max(scaled, axis=0, keepdims=True))
    neg = jnp.exp2(jnp.min(scaled, axis=0, keepdims=True) - scaled)
    return pos, neg, jnp.sum(pos, axis=0, keepdims=True), jnp.sum(neg, axis=0, keepdims=True)


def kernel(nc, nz, feats, q_hbm, k_hbm, v_hbm, qm_hbm, km_hbm, gain_ref, ri_hbm, out_ref,
           q_v, k_v, v_v, qm_v, km_v, ri_v, rit, gcol, fk, vta, pta, att, ssq, part,
           send_e, recv_e, send_p, recv_p, msg, got, red,
           tri, raw, tot, in_sem, s1, r1, s2, r2, s3, r3, s4, r4, *per_head):
    fq, wb = per_head[:len(per_head) // 2], per_head[len(per_head) // 2:]
    hl, kvl = qm_v.shape[0], km_v.shape[0]
    groups = hl // kvl
    rank = ri_v.shape[1]
    rb = rank // nz
    rows = send_e.shape[1]
    per = HD // rows
    mc, mz = lax.axis_index("ctx"), lax.axis_index("head")

    loads = [(k_hbm, k_v), (v_hbm, v_v), (km_hbm, km_v), (qm_hbm, qm_v),
             (q_hbm.at[0], q_v.at[0]), (ri_hbm, ri_v), (q_hbm.at[1], q_v.at[1])]
    loads = [pltpu.make_async_copy(a, b, in_sem.at[i]) for i, (a, b) in enumerate(loads)]
    for load in loads:
        load.start()

    barrier = pltpu.get_barrier_semaphore()

    def greet_ctx(i, _):
        pl.semaphore_signal(barrier, inc=1, device_id=(lax.rem(mc + i, nc), mz), device_id_type=MESH)
        return 0

    lax.fori_loop(1, nc, greet_ctx, 0)
    for i in range(1, nz):
        pl.semaphore_signal(barrier, inc=1, device_id=(mc, lax.rem(mz + i, nz)), device_id_type=MESH)

    for load in loads[:3]:
        load.wait()
    first = lax.broadcasted_iota(jnp.int32, (rows, HD), 0) == 0
    for s in range(SEQS):
        for g in range(kvl):
            i = s * kvl + g
            lanes = slice(g * HD, (g + 1) * HD)
            pos, neg, zp, zn = exps(tt(km_v[g], k_v[s, :, lanes]) * LOG2E)
            feat = jnp.concatenate([pos * (1.0 / zp), neg * (1.0 / zn)], axis=0).astype(bf16)
            fk[i] = feat.T
            vta[i, 0:HD, :] = v_v[s, :, lanes].T
            vta[i, HD:HD + 16, :] = jnp.ones((16, BLK), bf16)
            state = nn(vta[i], fk[i])
            for p in range(per):
                j = i * per + p
                send_e[j, :, 0:2 * HD] = state[p * rows:(p + 1) * rows].astype(bf16)
                send_e[j, :, 2 * HD:] = jnp.where(
                    first, state[HD:HD + 1, 0:HD], state[HD:HD + 1, HD:2 * HD]).astype(bf16)

    pl.semaphore_wait(barrier, nc - 1 + nz - 1)

    def exchange(src, dst, ssem, rsem, i):
        to = lax.rem(mc + i, nc)
        return pltpu.make_async_remote_copy(
            src_ref=src.at[to], dst_ref=dst.at[mc], send_sem=ssem, recv_sem=rsem,
            device_id=(to, mz), device_id_type=MESH)

    def arrivals(src, dst, ssem, rsem):
        return pltpu.make_async_remote_copy(
            src_ref=src.at[pl.ds(0, nc - 1)], dst_ref=dst.at[pl.ds(0, nc - 1)], send_sem=ssem, recv_sem=rsem,
            device_id=(lax.rem(mc + 1, nc), mz), device_id_type=MESH)

    for i in range(1, nc):
        exchange(send_e, recv_e, s1, r1, i).start()
    recv_e[mc] = send_e[mc]

    for load in loads[3:6]:
        load.wait()

    tri[...] = (lax.broadcasted_iota(jnp.int32, (HD, HD), 0)
                <= lax.broadcasted_iota(jnp.int32, (HD, HD), 1)).astype(f32).astype(bf16)

    ST, AT = raw.shape[0], tot.shape[0]

    def joined(ref, i):
        return jnp.concatenate([ref[i, 0], ref[i, 1]], axis=1)

    def lanes_of(h):
        return pl.ds(pl.multiple_of(h * HD, HD), HD)

    def dots(s, i, j):
        h = i * ST + j
        raw[j] = tt(qm_v[h], q_v[s, :, lanes_of(h)]) * LOG2E

    def features(s, i, j):
        at = s * (hl // ST) + i
        for c in range(BLK // HD):
            pos, neg, zp, zn = exps(raw[j, :, c * HD:(c + 1) * HD])
            fq[j][at, c, 0:HD, :] = pos.astype(bf16)
            fq[j][at, c, HD:, :] = (neg * (zp / zn)).astype(bf16)

    def weigh(s, i, j):
        at = s * (hl // ST) + i
        score = nn(fk[s * kvl + (i * ST + j) // groups], joined(fq[j], at))
        wb[j][at, 0, 0:HD, :] = score[0:HD, 0:HD].astype(bf16) * tri[...]
        wb[j][at, 1, 0:HD, :] = score[0:HD, HD:].astype(bf16)
        wb[j][at, 0, HD:, :] = jnp.zeros((HD, HD), bf16)
        wb[j][at, 1, HD:, :] = score[HD:, HD:].astype(bf16) * tri[...]

    def prepare(i, j):
        at = lanes_of(i * ST + j)
        gcol[i * ST + j] = jnp.broadcast_to(gain_ref[0:1, at].astype(f32), (HD, HD)).T
        rit[:, at] = ri_v[at, :].T

    def attend(s, i, j):
        g = s * kvl + (i * AT + j) // groups
        at = s * (hl // ST) + i * (AT // ST) + j // ST
        tot[j] = nn(vta[g], joined(wb[j % ST], at)) + nn(pta[g], joined(fq[j % ST], at))

    def divide(s, i, j):
        h = i * AT + j
        out = tot[j, 0:HD] * (1.0 / tot[j, HD:HD + 1])
        ssq[s] += jnp.sum((out * out).reshape(HD // 16, 16, BLK), axis=0)
        scale = gcol[h]
        att[s, lanes_of(h), :] = jnp.concatenate(
            [out[:, 0:HD] * scale, out[:, HD:] * scale], axis=1).astype(bf16)

    def heads(step, stages, extra=None):
        depth, count = len(stages) - 1, hl // step
        last = depth + (extra is not None)

        def trip(i, live):
            if extra is not None and last in live:
                extra(i - last)
            for j in range(step):
                for k in range(depth, -1, -1):
                    if k in live:
                        stages[k](i - k, j)

        for i in range(last):
            trip(i, range(0, i + 1))

        def run(i, _):
            trip(i, range(last + 1))
            return 0

        lax.fori_loop(last, count, run, 0)
        for i in range(count, count + last):
            trip(i, range(i - count + 1, last + 1))

    heads(ST, [lambda i, j: dots(0, i, j), lambda i, j: (features(0, i, j), prepare(i, j)),
               lambda i, j: weigh(0, i, j)])
    loads[6].wait()

    arrivals(send_e, recv_e, s1, r1).wait_recv()

    def scan(i, total):
        send_p[i] = total.astype(bf16)
        return total + recv_e[i].astype(f32)

    lax.fori_loop(0, nc, scan, jnp.zeros(send_p.shape[1:], f32))

    for i in range(1, nc):
        exchange(send_p, recv_p, s2, r2, i).start()
    recv_p[mc] = send_p[mc]

    heads(ST, [functools.partial(f, 1) for f in (dots, features, weigh)])

    arrivals(send_p, recv_p, s2, r2).wait_recv()
    for i in range(SEQS * kvl):
        for p in range(per):
            pta[i, p * rows:(p + 1) * rows, :] = recv_p[i * per + p, :, 0:2 * HD]
        sums = recv_p[i * per, 0:2, 2 * HD:].astype(f32)
        pta[i, HD:HD + 16, :] = jnp.broadcast_to(
            jnp.concatenate([sums[0:1], sums[1:2]], axis=1), (16, BLK)).astype(bf16)

    ssq[...] = jnp.zeros_like(ssq)

    def partner(s, i):
        return lax.rem(mz + i, nz)

    def scatter(s, i):
        to = lax.rem(mz + i, nz)
        return pltpu.make_async_remote_copy(
            src_ref=msg.at[s, i - 1], dst_ref=got.at[s, i - 1], send_sem=s3.at[s, i], recv_sem=r3.at[s, i],
            device_id=(mc, to), device_id_type=MESH)

    def gather(s, i, at):
        to = lax.rem(mz + i, nz)
        return pltpu.make_async_remote_copy(
            src_ref=red.at[s, at], dst_ref=red.at[s, at], send_sem=s4.at[s, i], recv_sem=r4.at[s, i],
            device_id=(mc, to), device_id_type=MESH)

    def project(s):
        for i in (2, 1, 3, 0) if nz == 4 else range(nz - 1, -1, -1):
            to = lax.rem(mz + i, nz)
            block = nn(rit[pl.ds(pl.multiple_of(to * rb, rb), rb), :], att[s])
            if i == 0:
                part[s] = block
            else:
                msg[s, i - 1, 0:rb, :] = block.astype(bf16)
                msg[s, i - 1, rb:, :] = ssq[s].astype(bf16)
                scatter(s, i).start()

    def reduce(s):
        for i in range(1, nz):
            scatter(s, i).wait_recv()
        total = part[s]
        squares = ssq[s]
        for i in range(1, nz):
            total = total + got[s, i - 1, 0:rb, :].astype(f32)
            squares = squares + got[s, i - 1, rb:, :].astype(f32)
        factor = lax.rsqrt(jnp.sum(squares, axis=0, keepdims=True) / feats + 1e-05)
        red[s, mz] = (total * factor).astype(bf16)
        for i in range(1, nz):
            gather(s, i, mz).start()

    heads(AT, [functools.partial(f, 0) for f in (attend, divide)])
    project(0)
    heads(AT, [functools.partial(f, 1) for f in (attend, divide)])
    reduce(0)
    project(1)
    reduce(1)
    for s in range(SEQS):
        for i in range(1, nz):
            gather(s, i, lax.rem(mz + nz - i, nz)).wait_recv()
        for p in range(nz):
            out_ref[s, :, p * rb:(p + 1) * rb] = red[s, p].T

    arrivals(send_e, recv_e, s1, r1).wait_send()
    arrivals(send_p, recv_p, s2, r2).wait_send()
    for s in range(SEQS):
        for i in range(1, nz):
            scatter(s, i).wait_send()
            gather(s, i, mz).wait_send()


def attention(nc, nz, q, k, v, qm, km, gain, ri):
    hl, kvl, rank = qm.shape[0], km.shape[0], ri.shape[1]
    rows = SEQS * kvl * HD // nc
    rb = rank // nz
    states = SEQS * kvl
    st, at = min(ST, hl), min(AT, hl)
    vm, dma = pltpu.VMEM, pltpu.SemaphoreType.DMA
    hbm = pl.BlockSpec(memory_space=pltpu.HBM)
    vmem = pl.BlockSpec(memory_space=pltpu.VMEM)
    return pl.pallas_call(
        functools.partial(kernel, nc, nz, float(nz * hl * HD)),
        out_shape=jax.ShapeDtypeStruct((SEQS, BLK, rank), bf16),
        in_specs=[hbm, hbm, hbm, hbm, hbm, vmem, hbm],
        out_specs=vmem,
        scratch_shapes=[
            vm(q.shape, bf16), vm(k.shape, bf16), vm(v.shape, bf16), vm(qm.shape, bf16),
            vm(km.shape, bf16), vm(ri.shape, bf16), vm((rank, hl * HD), bf16), vm((hl, HD, HD), f32),
            vm((states, BLK, 2 * HD), bf16), vm((states, HD + 16, BLK), bf16), vm((states, HD + 16, 2 * HD), bf16),
            vm((SEQS, hl * HD, BLK), bf16), vm((SEQS, 16, BLK), f32), vm((SEQS, rb, BLK), f32),
            vm((nc, rows, 3 * HD), bf16), vm((nc, rows, 3 * HD), bf16),
            vm((nc, rows, 3 * HD), bf16), vm((nc, rows, 3 * HD), bf16),
            vm((SEQS, nz - 1, rb + 16, BLK), bf16), vm((SEQS, nz - 1, rb + 16, BLK), bf16),
            vm((SEQS, nz, rb, BLK), bf16), vm((HD, HD), bf16),
            vm((st, HD, BLK), f32), vm((at, HD + 16, BLK), f32),
            dma((7,)), dma, dma, dma, dma,
            dma((SEQS, nz)), dma((SEQS, nz)), dma((SEQS, nz)), dma((SEQS, nz)),
        ] + [vm((SEQS * hl // st, 2, 2 * HD, HD), bf16)] * st + [
            vm((SEQS * hl // st, 2, BLK, HD), bf16)] * st + [
        ],
        compiler_params=pltpu.CompilerParams(
            collective_id=0, has_side_effects=True, vmem_limit_bytes=VLIM * 2**20),
        name="attention",
    )(q, k, v, qm, km, gain, ri)


def solution(mesh):
    nc, nz = mesh.shape["ctx"], mesh.shape["head"]

    def shards(queries, key_input, values, query_map, key_map, out_gain, rank_in, rank_out):
        reduced = attention(nc, nz, queries, key_input, values, query_map, key_map,
                            out_gain.reshape(1, -1), rank_in)
        return jnp.einsum('str,rn->stn', reduced, rank_out, preferred_element_type=f32).astype(bf16)

    in_specs = (
        P(None, "ctx", "head"),
        P(None, "ctx", "head"),
        P(None, "ctx", "head"),
        P("head", None, None),
        P("head", None, None),
        P("head"),
        P("head", None),
        P(None, "head"),
    )
    out_specs = P(None, "ctx", "head")
    return jax.shard_map(shards, mesh=mesh, in_specs=in_specs, out_specs=out_specs, check_vma=False)
```

```python
import functools

import jax
import jax.numpy as jnp
from jax import lax
from jax.experimental import pallas as pl
from jax.experimental.pallas import tpu as pltpu
from jax.sharding import PartitionSpec as P

HD = 128
BLK = 256
SEQS = 2
ST, AT = 8, 8
VLIM = 59
OUT_TILES = 4
LOG2E = 1.4426950408889634
MESH = pl.DeviceIdType.MESH
bf16, f32 = jnp.bfloat16, jnp.float32


def nn(a, b):
    return jnp.dot(a, b, preferred_element_type=f32)


def tt(a, b):
    return lax.dot_general(a, b, (((0,), (1,)), ((), ())), preferred_element_type=f32)


def exps(scaled):
    pos = jnp.exp2(scaled - jnp.max(scaled, axis=0, keepdims=True))
    neg = jnp.exp2(jnp.min(scaled, axis=0, keepdims=True) - scaled)
    return pos, neg, jnp.sum(pos, axis=0, keepdims=True), jnp.sum(neg, axis=0, keepdims=True)


def kernel(nc, nz, feats, q_hbm, k_hbm, v_hbm, qm_hbm, km_hbm, gain_ref, ri_hbm, ro_hbm, out_ref,
           q_v, k_v, v_v, qm_v, km_v, ri_v, ro_v, rit, gcol, gains, fk, vta, pta, att, ssq, part,
           send_e, recv_e, send_p, recv_p, msg, got, red,
           tri, raw, tot, in_sem, s1, r1, s2, r2, s3, r3, s4, r4, *per_head):
    fq, wb = per_head[:len(per_head) // 2], per_head[len(per_head) // 2:]
    hl, kvl = qm_v.shape[0], km_v.shape[0]
    groups = hl // kvl
    rank = ri_v.shape[1]
    rb = rank // nz
    rows = send_e.shape[1]
    per = HD // rows
    mc, mz = lax.axis_index("ctx"), lax.axis_index("head")

    loads = [(k_hbm, k_v), (v_hbm, v_v), (km_hbm, km_v), (qm_hbm, qm_v),
             (q_hbm.at[0], q_v.at[0]), (ri_hbm, ri_v), (q_hbm.at[1], q_v.at[1]), (ro_hbm, ro_v)]
    loads = [pltpu.make_async_copy(a, b, in_sem.at[i]) for i, (a, b) in enumerate(loads)]
    for load in loads:
        load.start()

    gains[...] = gain_ref[...].astype(f32)
    barrier = pltpu.get_barrier_semaphore()

    def greet_ctx(i, _):
        pl.semaphore_signal(barrier, inc=1, device_id=(lax.rem(mc + i, nc), mz), device_id_type=MESH)
        return 0

    lax.fori_loop(1, nc, greet_ctx, 0)
    for i in range(1, nz):
        pl.semaphore_signal(barrier, inc=1, device_id=(mc, lax.rem(mz + i, nz)), device_id_type=MESH)

    for load in loads[:3]:
        load.wait()
    first = lax.broadcasted_iota(jnp.int32, (rows, HD), 0) == 0
    for s in range(SEQS):
        for g in range(kvl):
            i = s * kvl + g
            lanes = slice(g * HD, (g + 1) * HD)
            pos, neg, zp, zn = exps(tt(km_v[g], k_v[s, :, lanes]) * LOG2E)
            feat = jnp.concatenate([pos * (1.0 / zp), neg * (1.0 / zn)], axis=0).astype(bf16)
            fk[i] = feat.T
            vta[i, 0:HD, :] = v_v[s, :, lanes].T
            vta[i, HD:HD + 16, :] = jnp.ones((16, BLK), bf16)
            state = nn(vta[i], fk[i])
            for p in range(per):
                j = i * per + p
                send_e[j, :, 0:2 * HD] = state[p * rows:(p + 1) * rows].astype(bf16)
                send_e[j, :, 2 * HD:] = jnp.where(
                    first, state[HD:HD + 1, 0:HD], state[HD:HD + 1, HD:2 * HD]).astype(bf16)

    pl.semaphore_wait(barrier, nc - 1 + nz - 1)

    def exchange(src, dst, ssem, rsem, i):
        to = lax.rem(mc + i, nc)
        return pltpu.make_async_remote_copy(
            src_ref=src.at[to], dst_ref=dst.at[mc], send_sem=ssem, recv_sem=rsem,
            device_id=(to, mz), device_id_type=MESH)

    def arrivals(src, dst, ssem, rsem):
        return pltpu.make_async_remote_copy(
            src_ref=src.at[pl.ds(0, nc - 1)], dst_ref=dst.at[pl.ds(0, nc - 1)], send_sem=ssem, recv_sem=rsem,
            device_id=(lax.rem(mc + 1, nc), mz), device_id_type=MESH)

    for i in range(1, nc):
        exchange(send_e, recv_e, s1, r1, i).start()
    recv_e[mc] = send_e[mc]

    for load in loads[3:6]:
        load.wait()

    tri[...] = (lax.broadcasted_iota(jnp.int32, (HD, HD), 0)
                <= lax.broadcasted_iota(jnp.int32, (HD, HD), 1)).astype(f32).astype(bf16)

    ST, AT = raw.shape[0], tot.shape[0]

    def joined(ref, i):
        return jnp.concatenate([ref[i, 0], ref[i, 1]], axis=1)

    def lanes_of(h):
        return pl.ds(pl.multiple_of(h * HD, HD), HD)

    def dots(s, i, j):
        h = i * ST + j
        raw[j] = tt(qm_v[h], q_v[s, :, lanes_of(h)]) * LOG2E

    def features(s, i, j):
        at = s * (hl // ST) + i
        for c in range(BLK // HD):
            pos, neg, zp, zn = exps(raw[j, :, c * HD:(c + 1) * HD])
            fq[j][at, c, 0:HD, :] = pos.astype(bf16)
            fq[j][at, c, HD:, :] = (neg * (zp / zn)).astype(bf16)

    def weigh(s, i, j):
        at = s * (hl // ST) + i
        score = nn(fk[s * kvl + (i * ST + j) // groups], joined(fq[j], at))
        wb[j][at, 0, 0:HD, :] = score[0:HD, 0:HD].astype(bf16) * tri[...]
        wb[j][at, 1, 0:HD, :] = score[0:HD, HD:].astype(bf16)
        wb[j][at, 0, HD:, :] = jnp.zeros((HD, HD), bf16)
        wb[j][at, 1, HD:, :] = score[HD:, HD:].astype(bf16) * tri[...]

    def prepare(i, j):
        at = lanes_of(i * ST + j)
        gcol[i * ST + j] = jnp.broadcast_to(gains[pl.ds(i * ST + j, 1), :], (HD, HD)).T
        rit[:, at] = ri_v[at, :].T

    def attend(s, i, j):
        g = s * kvl + (i * AT + j) // groups
        at = s * (hl // ST) + i * (AT // ST) + j // ST
        tot[j] = nn(vta[g], joined(wb[j % ST], at)) + nn(pta[g], joined(fq[j % ST], at))

    def divide(s, i, j):
        h = i * AT + j
        out = tot[j, 0:HD] * (1.0 / tot[j, HD:HD + 1])
        ssq[s] += jnp.sum((out * out).reshape(HD // 16, 16, BLK), axis=0)
        scale = gcol[h]
        att[s, lanes_of(h), :] = jnp.concatenate(
            [out[:, 0:HD] * scale, out[:, HD:] * scale], axis=1).astype(bf16)

    def heads(step, stages, extra=None):
        depth, count = len(stages) - 1, hl // step
        last = depth + (extra is not None)

        def trip(i, live):
            if extra is not None and last in live:
                extra(i - last)
            for j in range(step):
                for k in range(depth, -1, -1):
                    if k in live:
                        stages[k](i - k, j)

        for i in range(last):
            trip(i, range(0, i + 1))

        def run(i, _):
            trip(i, range(last + 1))
            return 0

        lax.fori_loop(last, count, run, 0)
        for i in range(count, count + last):
            trip(i, range(i - count + 1, last + 1))

    heads(ST, [lambda i, j: dots(0, i, j), lambda i, j: (features(0, i, j), prepare(i, j)),
               lambda i, j: weigh(0, i, j)])
    loads[6].wait()

    arrivals(send_e, recv_e, s1, r1).wait_recv()

    def scan(i, total):
        send_p[i] = total.astype(bf16)
        return total + recv_e[i].astype(f32)

    lax.fori_loop(0, nc, scan, jnp.zeros(send_p.shape[1:], f32))

    for i in range(1, nc):
        exchange(send_p, recv_p, s2, r2, i).start()
    recv_p[mc] = send_p[mc]

    heads(ST, [functools.partial(f, 1) for f in (dots, features, weigh)])

    arrivals(send_p, recv_p, s2, r2).wait_recv()
    for i in range(SEQS * kvl):
        for p in range(per):
            pta[i, p * rows:(p + 1) * rows, :] = recv_p[i * per + p, :, 0:2 * HD]
        sums = recv_p[i * per, 0:2, 2 * HD:].astype(f32)
        pta[i, HD:HD + 16, :] = jnp.broadcast_to(
            jnp.concatenate([sums[0:1], sums[1:2]], axis=1), (16, BLK)).astype(bf16)

    ssq[...] = jnp.zeros_like(ssq)

    def partner(s, i):
        return lax.rem(mz + i, nz)

    def scatter(s, i):
        to = lax.rem(mz + i, nz)
        return pltpu.make_async_remote_copy(
            src_ref=msg.at[s, i - 1], dst_ref=got.at[s, i - 1], send_sem=s3.at[s, i], recv_sem=r3.at[s, i],
            device_id=(mc, to), device_id_type=MESH)

    def gather(s, i, at):
        to = lax.rem(mz + i, nz)
        return pltpu.make_async_remote_copy(
            src_ref=red.at[s, at], dst_ref=red.at[s, at], send_sem=s4.at[s, i], recv_sem=r4.at[s, i],
            device_id=(mc, to), device_id_type=MESH)

    def project(s):
        for i in (2, 1, 3, 0) if nz == 4 else range(nz - 1, -1, -1):
            to = lax.rem(mz + i, nz)
            block = nn(rit[pl.ds(pl.multiple_of(to * rb, rb), rb), :], att[s])
            if i == 0:
                part[s] = block
            else:
                msg[s, i - 1, 0:rb, :] = block.astype(bf16)
                msg[s, i - 1, rb:, :] = ssq[s].astype(bf16)
                scatter(s, i).start()

    def reduce(s):
        for i in range(1, nz):
            scatter(s, i).wait_recv()
        total = part[s]
        squares = ssq[s]
        for i in range(1, nz):
            total = total + got[s, i - 1, 0:rb, :].astype(f32)
            squares = squares + got[s, i - 1, rb:, :].astype(f32)
        factor = lax.rsqrt(jnp.sum(squares, axis=0, keepdims=True) / feats + 1e-05)
        red[s, mz] = (total * factor).astype(bf16)
        for i in range(1, nz):
            gather(s, i, mz).start()

    def expand(s):
        for i in range(1, nz):
            gather(s, i, lax.rem(mz + nz - i, nz)).wait_recv()
        lhs = jnp.concatenate([red[s, p].T for p in range(nz)], axis=1)
        tile = out_ref.shape[2] // OUT_TILES
        for n in range(OUT_TILES):
            cols = slice(n * tile, (n + 1) * tile)
            out_ref[s, :, cols] = nn(lhs, ro_v[:, cols]).astype(bf16)

    heads(AT, [functools.partial(f, 0) for f in (attend, divide)])
    project(0)
    heads(AT, [functools.partial(f, 1) for f in (attend, divide)])
    reduce(0)
    project(1)
    loads[7].wait()
    expand(0)
    reduce(1)
    expand(1)
    arrivals(send_e, recv_e, s1, r1).wait_send()
    arrivals(send_p, recv_p, s2, r2).wait_send()
    for s in range(SEQS):
        for i in range(1, nz):
            scatter(s, i).wait_send()
            gather(s, i, mz).wait_send()


def attention(nc, nz, q, k, v, qm, km, gain, ri, ro):
    hl, kvl, rank = qm.shape[0], km.shape[0], ri.shape[1]
    rows = SEQS * kvl * HD // nc
    rb = rank // nz
    states = SEQS * kvl
    st, at = min(ST, hl), min(AT, hl)
    vm, dma = pltpu.VMEM, pltpu.SemaphoreType.DMA
    hbm = pl.BlockSpec(memory_space=pltpu.HBM)
    vmem = pl.BlockSpec(memory_space=pltpu.VMEM)
    return pl.pallas_call(
        functools.partial(kernel, nc, nz, float(nz * hl * HD)),
        out_shape=pltpu.VMEM(q.shape, bf16),
        in_specs=[hbm, hbm, hbm, hbm, hbm, vmem, hbm, hbm],
        out_specs=pl.BlockSpec(memory_space=pltpu.VMEM),
        scratch_shapes=[
            vm(q.shape, bf16), vm(k.shape, bf16), vm(v.shape, bf16), vm(qm.shape, bf16),
            vm(km.shape, bf16), vm(ri.shape, bf16), vm(ro.shape, bf16),
            vm((rank, hl * HD), bf16), vm((hl, HD, HD), f32), vm((hl, HD), f32),
            vm((states, BLK, 2 * HD), bf16), vm((states, HD + 16, BLK), bf16), vm((states, HD + 16, 2 * HD), bf16),
            vm((SEQS, hl * HD, BLK), bf16), vm((SEQS, 16, BLK), f32), vm((SEQS, rb, BLK), f32),
            vm((nc, rows, 3 * HD), bf16), vm((nc, rows, 3 * HD), bf16),
            vm((nc, rows, 3 * HD), bf16), vm((nc, rows, 3 * HD), bf16),
            vm((SEQS, nz - 1, rb + 16, BLK), bf16), vm((SEQS, nz - 1, rb + 16, BLK), bf16),
            vm((SEQS, nz, rb, BLK), bf16), vm((HD, HD), bf16),
            vm((st, HD, BLK), f32), vm((at, HD + 16, BLK), f32),
            dma((8,)), dma, dma, dma, dma,
            dma((SEQS, nz)), dma((SEQS, nz)), dma((SEQS, nz)), dma((SEQS, nz)),
        ] + [vm((SEQS * hl // st, 2, 2 * HD, HD), bf16)] * st + [
            vm((SEQS * hl // st, 2, BLK, HD), bf16)] * st + [
        ],
        compiler_params=pltpu.CompilerParams(
            collective_id=0, has_side_effects=True, vmem_limit_bytes=VLIM * 2**20),
        name="attention",
    )(q, k, v, qm, km, gain, ri, ro)


def solution(mesh):
    nc, nz = mesh.shape["ctx"], mesh.shape["head"]

    def shards(queries, key_input, values, query_map, key_map, out_gain, rank_in, rank_out):
        return attention(nc, nz, queries, key_input, values, query_map, key_map,
                         out_gain.reshape(-1, HD), rank_in, rank_out)

    in_specs = (
        P(None, "ctx", "head"),
        P(None, "ctx", "head"),
        P(None, "ctx", "head"),
        P("head", None, None),
        P("head", None, None),
        P("head"),
        P("head", None),
        P(None, "head"),
    )
    out_specs = P(None, "ctx", "head")
    return jax.shard_map(shards, mesh=mesh, in_specs=in_specs, out_specs=out_specs, check_vma=False)
```

```python
import functools

import jax
import jax.numpy as jnp
from jax import lax
from jax.experimental import pallas as pl
from jax.experimental.pallas import tpu as pltpu
from jax.sharding import PartitionSpec as P

HD = 128
BLK = 256
SEQS = 2
ST = 8
VLIM = 59
OUT_TILES = 4
LOG2E = 1.4426950408889634
MESH = pl.DeviceIdType.MESH
bf16, f32 = jnp.bfloat16, jnp.float32


def nn(a, b):
    return jnp.dot(a, b, preferred_element_type=f32)


def tt(a, b):
    return lax.dot_general(a, b, (((0,), (1,)), ((), ())), preferred_element_type=f32)


def exps(scaled):
    pos = jnp.exp2(scaled - jnp.max(scaled, axis=0, keepdims=True))
    neg = jnp.exp2(jnp.min(scaled, axis=0, keepdims=True) - scaled)
    return pos, neg, jnp.sum(pos, axis=0, keepdims=True), jnp.sum(neg, axis=0, keepdims=True)


def kernel(nc, nz, feats, q_hbm, k_hbm, v_hbm, qm_hbm, km_hbm, gain_ref, ri_hbm, ro_hbm, out_ref,
           q_v, k_v, v_v, qm_v, km_v, ri_v, ro_v, rit, gcol, gains, fk, vta, pta, att, ssq, part,
           send_e, recv_e, send_p, recv_p, msg, got, red,
           tri, raw, tot, near, in_sem, s1, r1, s2, r2, s3, r3, s4, r4, *per_head):
    n = len(per_head) // 3
    fq, wb, loc = per_head[:n], per_head[n:2 * n], per_head[2 * n:]
    hl, kvl = qm_v.shape[0], km_v.shape[0]
    groups = hl // kvl
    rank = ri_v.shape[1]
    rb = rank // nz
    rows = send_e.shape[1]
    per = HD // rows
    mc, mz = lax.axis_index("ctx"), lax.axis_index("head")

    loads = [(k_hbm, k_v), (v_hbm, v_v), (km_hbm, km_v), (qm_hbm, qm_v),
             (q_hbm.at[0], q_v.at[0]), (ri_hbm, ri_v), (q_hbm.at[1], q_v.at[1]), (ro_hbm, ro_v)]
    loads = [pltpu.make_async_copy(a, b, in_sem.at[i]) for i, (a, b) in enumerate(loads)]
    for load in loads:
        load.start()

    gains[...] = gain_ref[...].astype(f32)
    barrier = pltpu.get_barrier_semaphore()

    def greet_ctx(i, _):
        pl.semaphore_signal(barrier, inc=1, device_id=(lax.rem(mc + i, nc), mz), device_id_type=MESH)
        return 0

    lax.fori_loop(1, nc, greet_ctx, 0)
    for i in range(1, nz):
        pl.semaphore_signal(barrier, inc=1, device_id=(mc, lax.rem(mz + i, nz)), device_id_type=MESH)

    for load in loads[:3]:
        load.wait()
    first = lax.broadcasted_iota(jnp.int32, (rows, HD), 0) == 0
    for s in range(SEQS):
        for g in range(kvl):
            i = s * kvl + g
            lanes = slice(g * HD, (g + 1) * HD)
            pos, neg, zp, zn = exps(tt(km_v[g], k_v[s, :, lanes]) * LOG2E)
            feat = jnp.concatenate([pos * (1.0 / zp), neg * (1.0 / zn)], axis=0).astype(bf16)
            fk[i] = feat.T
            vta[i, 0:HD, :] = v_v[s, :, lanes].T
            vta[i, HD:HD + 16, :] = jnp.ones((16, BLK), bf16)
            state = nn(vta[i], fk[i])
            for p in range(per):
                j = i * per + p
                send_e[j, :, 0:2 * HD] = state[p * rows:(p + 1) * rows].astype(bf16)
                send_e[j, :, 2 * HD:] = jnp.where(
                    first, state[HD:HD + 1, 0:HD], state[HD:HD + 1, HD:2 * HD]).astype(bf16)

    pl.semaphore_wait(barrier, nc - 1 + nz - 1)

    def exchange(src, dst, ssem, rsem, i):
        to = lax.rem(mc + i, nc)
        return pltpu.make_async_remote_copy(
            src_ref=src.at[to], dst_ref=dst.at[mc], send_sem=ssem, recv_sem=rsem,
            device_id=(to, mz), device_id_type=MESH)

    def arrivals(src, dst, ssem, rsem):
        return pltpu.make_async_remote_copy(
            src_ref=src.at[pl.ds(0, nc - 1)], dst_ref=dst.at[pl.ds(0, nc - 1)], send_sem=ssem, recv_sem=rsem,
            device_id=(lax.rem(mc + 1, nc), mz), device_id_type=MESH)

    for i in range(1, nc):
        exchange(send_e, recv_e, s1, r1, i).start()
    recv_e[mc] = send_e[mc]

    for load in loads[3:6]:
        load.wait()

    tri[...] = (lax.broadcasted_iota(jnp.int32, (HD, HD), 0)
                <= lax.broadcasted_iota(jnp.int32, (HD, HD), 1)).astype(f32).astype(bf16)

    ST = raw.shape[0]

    def joined(ref, i):
        return jnp.concatenate([ref[i, 0], ref[i, 1]], axis=1)

    def lanes_of(h):
        return pl.ds(pl.multiple_of(h * HD, HD), HD)

    def dots(s, i, j):
        h = i * ST + j
        raw[j] = tt(qm_v[h], q_v[s, :, lanes_of(h)]) * LOG2E

    def features(s, i, j):
        at = s * (hl // ST) + i
        for c in range(BLK // HD):
            pos, neg, zp, zn = exps(raw[j, :, c * HD:(c + 1) * HD])
            fq[j][at, c, 0:HD, :] = pos.astype(bf16)
            fq[j][at, c, HD:, :] = (neg * (zp / zn)).astype(bf16)

    def weigh(s, i, j):
        at = s * (hl // ST) + i
        score = nn(fk[s * kvl + (i * ST + j) // groups], joined(fq[j], at))
        wb[j][at, 0, 0:HD, :] = score[0:HD, 0:HD].astype(bf16) * tri[...]
        wb[j][at, 1, 0:HD, :] = score[0:HD, HD:].astype(bf16)
        wb[j][at, 0, HD:, :] = jnp.zeros((HD, HD), bf16)
        wb[j][at, 1, HD:, :] = score[HD:, HD:].astype(bf16) * tri[...]

    def prepare(i, j):
        at = lanes_of(i * ST + j)
        gcol[i * ST + j] = jnp.broadcast_to(gains[pl.ds(i * ST + j, 1), :], (HD, HD)).T
        rit[:, at] = ri_v[at, :].T

    def local(s, i, j):
        loc[j][i] = nn(vta[s * kvl + (i * ST + j) // groups], joined(wb[j], s * (hl // ST) + i))

    def attend(s, i, j):
        tot[j] = loc[j][i] + nn(pta[s * kvl + (i * ST + j) // groups], joined(fq[j], s * (hl // ST) + i))

    def divide(s, i, j):
        h = i * ST + j
        out = tot[j, 0:HD] * (1.0 / tot[j, HD:HD + 1])
        ssq[s] += jnp.sum((out * out).reshape(HD // 16, 16, BLK), axis=0)
        scale = gcol[h]
        att[s, lanes_of(h), :] = jnp.concatenate(
            [out[:, 0:HD] * scale, out[:, HD:] * scale], axis=1).astype(bf16)

    def heads(step, stages, hook=None):
        last, count = len(stages) - 1, hl // step

        def trip(i, live):
            for j in range(step):
                for k in range(last, -1, -1):
                    if k in live:
                        stages[k](i - k, j)

        def run(i, _):
            trip(i, range(last + 1))
            return 0

        for i in range(last):
            trip(i, range(0, i + 1))
        if hook is None:
            lax.fori_loop(last, count, run, 0)
        else:
            lax.fori_loop(last, hook[0], run, 0)
            hook[1]()
            lax.fori_loop(hook[0], count, run, 0)
        for i in range(count, count + last):
            trip(i, range(i - count + 1, last + 1))

    heads(ST, [lambda i, j: dots(0, i, j), lambda i, j: (features(0, i, j), prepare(i, j)),
               lambda i, j: weigh(0, i, j)])
    loads[6].wait()

    arrivals(send_e, recv_e, s1, r1).wait_recv()

    def scan(i, total):
        send_p[i] = total.astype(bf16)
        return total + recv_e[i].astype(f32)

    lax.fori_loop(0, nc, scan, jnp.zeros(send_p.shape[1:], f32))

    for i in range(1, nc):
        exchange(send_p, recv_p, s2, r2, i).start()
    recv_p[mc] = send_p[mc]

    heads(ST, [lambda i, j: (dots(1, i, j), local(0, i, j)), functools.partial(features, 1),
               functools.partial(weigh, 1)])

    arrivals(send_p, recv_p, s2, r2).wait_recv()
    for i in range(SEQS * kvl):
        for p in range(per):
            pta[i, p * rows:(p + 1) * rows, :] = recv_p[i * per + p, :, 0:2 * HD]
        sums = recv_p[i * per, 0:2, 2 * HD:].astype(f32)
        pta[i, HD:HD + 16, :] = jnp.broadcast_to(
            jnp.concatenate([sums[0:1], sums[1:2]], axis=1), (16, BLK)).astype(bf16)

    ssq[...] = jnp.zeros_like(ssq)

    up, far, down = (lax.rem(mz + i, nz) for i in (1, 2, 3))

    def hop(s, m):
        return pltpu.make_async_remote_copy(
            src_ref=msg.at[s, m], dst_ref=got.at[s, m], send_sem=s3.at[s, m], recv_sem=r3.at[s, m],
            device_id=(mc, up if m % 2 == 0 else down), device_id_type=MESH)

    def spread(s, m, owner, half):
        return pltpu.make_async_remote_copy(
            src_ref=red.at[s, owner, half], dst_ref=red.at[s, owner, half], send_sem=s4.at[s, m],
            recv_sem=r4.at[s, m], device_id=(mc, up if m % 2 == 0 else down), device_id_type=MESH)

    leaving = ((mz, 0), (mz, 1), (mz, 1), (mz, 0), (down, 0), (up, 1))
    coming = ((down, 0), (up, 1), (down, 1), (up, 0), (far, 0), (far, 1))

    def send(s, m, value):
        msg[s, m] = value.astype(bf16)
        hop(s, m).start()

    def project(s, between=None):
        for i in (2, 1, 3, 0):
            to = lax.rem(mz + i, nz)
            block = nn(rit[pl.ds(pl.multiple_of(to * rb, rb), rb), :], att[s])
            block = jnp.concatenate([block, ssq[s]], axis=0)
            low, high = block[:, 0:HD], block[:, HD:]
            if i == 2:
                send(s, 0, low)
                send(s, 1, high)
                if between is not None:
                    between()
            elif i == 1:
                send(s, 2, high)
                near[s, 0] = low
            elif i == 3:
                send(s, 3, low)
                near[s, 1] = high
            else:
                part[s] = block

    def relay(s):
        for m in range(2):
            hop(s, m).wait_recv()
            send(s, 4 + m, near[s, m] + got[s, m].astype(f32))

    def reduce(s):
        for half, ms in enumerate(((3, 4), (2, 5))):
            total = part[s, :, half * HD:(half + 1) * HD]
            for m in ms:
                hop(s, m).wait_recv()
                total = total + got[s, m].astype(f32)
            factor = lax.rsqrt(jnp.sum(total[rb:], axis=0, keepdims=True) / feats + 1e-05)
            red[s, mz, half] = (total[0:rb] * factor).astype(bf16)
            spread(s, half, *leaving[half]).start()
        for m in (2, 3):
            spread(s, m, *leaving[m]).start()

    def forward(s):
        for m in range(2):
            spread(s, m, *coming[m]).wait_recv()
            spread(s, 4 + m, *leaving[4 + m]).start()

    def expand(s):
        for m in range(2, 6):
            spread(s, m, *coming[m]).wait_recv()
        lhs = jnp.concatenate([jnp.concatenate([red[s, p, half].T for p in range(nz)], axis=1)
                               for half in range(2)], axis=0)
        tile = out_ref.shape[2] // OUT_TILES
        for n in range(OUT_TILES):
            cols = slice(n * tile, (n + 1) * tile)
            out_ref[s, :, cols] = nn(lhs, ro_v[:, cols]).astype(bf16)

    heads(ST, [lambda i, j: (attend(0, i, j), local(1, i, j)), functools.partial(divide, 0)])
    project(0)
    heads(ST, [functools.partial(f, 1) for f in (attend, divide)], hook=(2, lambda: relay(0)))
    project(1, lambda: reduce(0))
    relay(1)
    forward(0)
    loads[7].wait()
    reduce(1)
    expand(0)
    forward(1)
    expand(1)
    arrivals(send_e, recv_e, s1, r1).wait_send()
    arrivals(send_p, recv_p, s2, r2).wait_send()
    for s in range(SEQS):
        for m in range(6):
            hop(s, m).wait_send()
            spread(s, m, *leaving[m]).wait_send()


def attention(nc, nz, q, k, v, qm, km, gain, ri, ro):
    hl, kvl, rank = qm.shape[0], km.shape[0], ri.shape[1]
    rows = SEQS * kvl * HD // nc
    rb = rank // nz
    states = SEQS * kvl
    st = min(ST, hl)
    vm, dma = pltpu.VMEM, pltpu.SemaphoreType.DMA
    hbm = pl.BlockSpec(memory_space=pltpu.HBM)
    vmem = pl.BlockSpec(memory_space=pltpu.VMEM)
    return pl.pallas_call(
        functools.partial(kernel, nc, nz, float(nz * hl * HD)),
        out_shape=pltpu.VMEM(q.shape, bf16),
        in_specs=[hbm, hbm, hbm, hbm, hbm, vmem, hbm, hbm],
        out_specs=pl.BlockSpec(memory_space=pltpu.VMEM),
        scratch_shapes=[
            vm(q.shape, bf16), vm(k.shape, bf16), vm(v.shape, bf16), vm(qm.shape, bf16),
            vm(km.shape, bf16), vm(ri.shape, bf16), vm(ro.shape, bf16),
            vm((rank, hl * HD), bf16), vm((hl, HD, HD), f32), vm((hl, HD), f32),
            vm((states, BLK, 2 * HD), bf16), vm((states, HD + 16, BLK), bf16), vm((states, HD + 16, 2 * HD), bf16),
            vm((SEQS, hl * HD, BLK), bf16), vm((SEQS, 16, BLK), f32), vm((SEQS, rb + 16, BLK), f32),
            vm((nc, rows, 3 * HD), bf16), vm((nc, rows, 3 * HD), bf16),
            vm((nc, rows, 3 * HD), bf16), vm((nc, rows, 3 * HD), bf16),
            vm((SEQS, 6, rb + 16, HD), bf16), vm((SEQS, 6, rb + 16, HD), bf16),
            vm((SEQS, nz, 2, rb, HD), bf16), vm((HD, HD), bf16),
            vm((st, HD, BLK), f32), vm((st, HD + 16, BLK), f32), vm((SEQS, 2, rb + 16, HD), f32),
            dma((8,)), dma, dma, dma, dma,
            dma((SEQS, 6)), dma((SEQS, 6)), dma((SEQS, 6)), dma((SEQS, 6)),
        ] + [vm((SEQS * hl // st, 2, 2 * HD, HD), bf16)] * st + [
            vm((SEQS * hl // st, 2, BLK, HD), bf16)] * st + [vm((hl // st, HD + 16, BLK), f32)] * st,
        compiler_params=pltpu.CompilerParams(
            collective_id=0, has_side_effects=True, vmem_limit_bytes=VLIM * 2**20),
        name="attention",
    )(q, k, v, qm, km, gain, ri, ro)


def solution(mesh):
    nc, nz = mesh.shape["ctx"], mesh.shape["head"]

    def shards(queries, key_input, values, query_map, key_map, out_gain, rank_in, rank_out):
        return attention(nc, nz, queries, key_input, values, query_map, key_map,
                         out_gain.reshape(-1, HD), rank_in, rank_out)

    in_specs = (
        P(None, "ctx", "head"),
        P(None, "ctx", "head"),
        P(None, "ctx", "head"),
        P("head", None, None),
        P("head", None, None),
        P("head"),
        P("head", None),
        P(None, "head"),
    )
    out_specs = P(None, "ctx", "head")
    return jax.shard_map(shards, mesh=mesh, in_specs=in_specs, out_specs=out_specs, check_vma=False)
```

```python
import functools

import jax
import jax.numpy as jnp
from jax import lax
from jax.experimental import pallas as pl
from jax.experimental.pallas import tpu as pltpu
from jax.sharding import PartitionSpec as P

HD = 128
BLK = 256
SEQS = 2
ST = 8
VLIM = 59
OUT_TILES = 4
LOG2E = 1.4426950408889634
MESH = pl.DeviceIdType.MESH
bf16, f32 = jnp.bfloat16, jnp.float32


def nn(a, b):
    return jnp.dot(a, b, preferred_element_type=f32)


def tt(a, b):
    return lax.dot_general(a, b, (((0,), (1,)), ((), ())), preferred_element_type=f32)


def exps(scaled):
    pos = jnp.exp2(scaled - jnp.max(scaled, axis=0, keepdims=True))
    neg = jnp.exp2(jnp.min(scaled, axis=0, keepdims=True) - scaled)
    return pos, neg, jnp.sum(pos, axis=0, keepdims=True), jnp.sum(neg, axis=0, keepdims=True)


def kernel(nc, nz, feats, q_hbm, k_hbm, v_hbm, qm_hbm, km_hbm, gain_ref, ri_hbm, ro_hbm, out_ref,
           q_v, k_v, v_v, qm_v, km_v, ri_v, ro_v, rit, gcol, gains, fk, vta, pta, att, ssq, part,
           send_e, recv_e, send_p, recv_p, msg, got, red,
           tri, raw, tot, in_sem, s1, r1, s2, r2, s3, r3, s4, r4, *per_head):
    n = len(per_head) // 3
    fq, wb, loc = per_head[:n], per_head[n:2 * n], per_head[2 * n:]
    hl, kvl = qm_v.shape[0], km_v.shape[0]
    groups = hl // kvl
    rank = ri_v.shape[1]
    rb = rank // nz
    rows = send_e.shape[1]
    per = HD // rows
    mc, mz = lax.axis_index("ctx"), lax.axis_index("head")

    loads = [(k_hbm, k_v), (v_hbm, v_v), (km_hbm, km_v), (qm_hbm, qm_v),
             (q_hbm.at[0], q_v.at[0]), (ri_hbm, ri_v), (q_hbm.at[1], q_v.at[1]), (ro_hbm, ro_v)]
    loads = [pltpu.make_async_copy(a, b, in_sem.at[i]) for i, (a, b) in enumerate(loads)]
    for load in loads:
        load.start()

    gains[...] = gain_ref[...].astype(f32)
    barrier = pltpu.get_barrier_semaphore()

    def greet_ctx(i, _):
        pl.semaphore_signal(barrier, inc=1, device_id=(lax.rem(mc + i, nc), mz), device_id_type=MESH)
        return 0

    lax.fori_loop(1, nc, greet_ctx, 0)
    for i in range(1, nz):
        pl.semaphore_signal(barrier, inc=1, device_id=(mc, lax.rem(mz + i, nz)), device_id_type=MESH)

    for load in loads[:3]:
        load.wait()
    first = lax.broadcasted_iota(jnp.int32, (rows, HD), 0) == 0
    for s in range(SEQS):
        for g in range(kvl):
            i = s * kvl + g
            lanes = slice(g * HD, (g + 1) * HD)
            pos, neg, zp, zn = exps(tt(km_v[g], k_v[s, :, lanes]) * LOG2E)
            feat = jnp.concatenate([pos * (1.0 / zp), neg * (1.0 / zn)], axis=0).astype(bf16)
            fk[i] = feat.T
            vta[i, 0:HD, :] = v_v[s, :, lanes].T
            vta[i, HD:HD + 16, :] = jnp.ones((16, BLK), bf16)
            state = nn(vta[i], fk[i])
            for p in range(per):
                j = i * per + p
                send_e[j, :, 0:2 * HD] = state[p * rows:(p + 1) * rows].astype(bf16)
                send_e[j, :, 2 * HD:] = jnp.where(
                    first, state[HD:HD + 1, 0:HD], state[HD:HD + 1, HD:2 * HD]).astype(bf16)

    pl.semaphore_wait(barrier, nc - 1 + nz - 1)

    def exchange(src, dst, ssem, rsem, i):
        to = lax.rem(mc + i, nc)
        return pltpu.make_async_remote_copy(
            src_ref=src.at[to], dst_ref=dst.at[mc], send_sem=ssem, recv_sem=rsem,
            device_id=(to, mz), device_id_type=MESH)

    def arrivals(src, dst, ssem, rsem):
        return pltpu.make_async_remote_copy(
            src_ref=src.at[pl.ds(0, nc - 1)], dst_ref=dst.at[pl.ds(0, nc - 1)], send_sem=ssem, recv_sem=rsem,
            device_id=(lax.rem(mc + 1, nc), mz), device_id_type=MESH)

    for i in range(1, nc):
        exchange(send_e, recv_e, s1, r1, i).start()
    recv_e[mc] = send_e[mc]

    for load in loads[3:6]:
        load.wait()

    tri[...] = (lax.broadcasted_iota(jnp.int32, (HD, HD), 0)
                <= lax.broadcasted_iota(jnp.int32, (HD, HD), 1)).astype(f32).astype(bf16)

    ST = raw.shape[0]

    def joined(ref, i):
        return jnp.concatenate([ref[i, 0], ref[i, 1]], axis=1)

    def lanes_of(h):
        return pl.ds(pl.multiple_of(h * HD, HD), HD)

    def dots(s, i, j):
        h = i * ST + j
        raw[j] = tt(qm_v[h], q_v[s, :, lanes_of(h)]) * LOG2E

    def features(s, i, j):
        at = s * (hl // ST) + i
        for c in range(BLK // HD):
            pos, neg, zp, zn = exps(raw[j, :, c * HD:(c + 1) * HD])
            fq[j][at, c, 0:HD, :] = pos.astype(bf16)
            fq[j][at, c, HD:, :] = (neg * (zp / zn)).astype(bf16)

    def weigh(s, i, j):
        at = s * (hl // ST) + i
        score = nn(fk[s * kvl + (i * ST + j) // groups], joined(fq[j], at))
        wb[j][at, 0, 0:HD, :] = score[0:HD, 0:HD].astype(bf16) * tri[...]
        wb[j][at, 1, 0:HD, :] = score[0:HD, HD:].astype(bf16)
        wb[j][at, 0, HD:, :] = jnp.zeros((HD, HD), bf16)
        wb[j][at, 1, HD:, :] = score[HD:, HD:].astype(bf16) * tri[...]

    def prepare(i, j):
        at = lanes_of(i * ST + j)
        gcol[i * ST + j] = jnp.broadcast_to(gains[pl.ds(i * ST + j, 1), :], (HD, HD)).T
        rit[:, at] = ri_v[at, :].T

    def local(s, i, j):
        loc[j][i] = nn(vta[s * kvl + (i * ST + j) // groups], joined(wb[j], s * (hl // ST) + i))

    def attend(s, i, j):
        tot[j] = loc[j][i] + nn(pta[s * kvl + (i * ST + j) // groups], joined(fq[j], s * (hl // ST) + i))

    def attend_half(s, c, i, j):
        lanes = slice(c * HD, (c + 1) * HD)
        tot[j, :, lanes] = loc[j][i, :, lanes] + nn(
            pta[s * kvl + (i * ST + j) // groups], fq[j][s * (hl // ST) + i, c])

    def divide(s, cs, i, j):
        h = i * ST + j
        scale = gcol[h]
        for c in cs:
            lanes = slice(c * HD, (c + 1) * HD)
            out = tot[j, 0:HD, lanes] * (1.0 / tot[j, HD:HD + 1, lanes])
            ssq[s, :, lanes] += jnp.sum((out * out).reshape(HD // 16, 16, HD), axis=0)
            att[s, c, lanes_of(h), :] = (out * scale).astype(bf16)

    def heads(step, stages, hook=None):
        last, count = len(stages) - 1, hl // step

        def trip(i, live):
            for j in range(step):
                for k in range(last, -1, -1):
                    if k in live:
                        stages[k](i - k, j)

        def run(i, _):
            trip(i, range(last + 1))
            return 0

        for i in range(last):
            trip(i, range(0, i + 1))
        if hook is None:
            lax.fori_loop(last, count, run, 0)
        else:
            lax.fori_loop(last, hook[0], run, 0)
            hook[1]()
            lax.fori_loop(hook[0], count, run, 0)
        for i in range(count, count + last):
            trip(i, range(i - count + 1, last + 1))

    heads(ST, [lambda i, j: dots(0, i, j), lambda i, j: (features(0, i, j), prepare(i, j)),
               lambda i, j: weigh(0, i, j)])
    loads[6].wait()

    arrivals(send_e, recv_e, s1, r1).wait_recv()

    def scan(i, total):
        send_p[i] = total.astype(bf16)
        return total + recv_e[i].astype(f32)

    lax.fori_loop(0, nc, scan, jnp.zeros(send_p.shape[1:], f32))

    for i in range(1, nc):
        exchange(send_p, recv_p, s2, r2, i).start()
    recv_p[mc] = send_p[mc]

    heads(ST, [lambda i, j: (dots(1, i, j), local(0, i, j)), functools.partial(features, 1),
               functools.partial(weigh, 1)])

    arrivals(send_p, recv_p, s2, r2).wait_recv()
    for i in range(SEQS * kvl):
        for p in range(per):
            pta[i, p * rows:(p + 1) * rows, :] = recv_p[i * per + p, :, 0:2 * HD]
        sums = recv_p[i * per, 0:2, 2 * HD:].astype(f32)
        pta[i, HD:HD + 16, :] = jnp.broadcast_to(
            jnp.concatenate([sums[0:1], sums[1:2]], axis=1), (16, BLK)).astype(bf16)

    ssq[...] = jnp.zeros_like(ssq)

    def scatter(s, c, i):
        to = lax.rem(mz + i, nz)
        return pltpu.make_async_remote_copy(
            src_ref=msg.at[s, c, i - 1], dst_ref=got.at[s, c, i - 1], send_sem=s3.at[2 * s + c, i],
            recv_sem=r3.at[2 * s + c, i], device_id=(mc, to), device_id_type=MESH)

    def gather(s, c, i, at):
        to = lax.rem(mz + i, nz)
        return pltpu.make_async_remote_copy(
            src_ref=red.at[s, at, c], dst_ref=red.at[s, at, c], send_sem=s4.at[2 * s + c, i],
            recv_sem=r4.at[2 * s + c, i], device_id=(mc, to), device_id_type=MESH)

    order = (2, 1, 3)
    half = (slice(0, HD), slice(HD, BLK))

    def project(s, cs):
        rhs = jnp.concatenate([att[s, c] for c in cs], axis=1)
        for i in order + (0,):
            to = lax.rem(mz + i, nz)
            block = nn(rit[pl.ds(pl.multiple_of(to * rb, rb), rb), :], rhs)
            for n, c in enumerate(cs):
                piece = jnp.concatenate([block[:, n * HD:(n + 1) * HD], ssq[s, :, half[c]]], axis=0)
                if i == 0:
                    part[s, :, half[c]] = piece
                else:
                    msg[s, c, i - 1] = piece.astype(bf16)
                    scatter(s, c, i).start()

    def reduce(s, c):
        total = part[s, :, half[c]]
        for i in order:
            scatter(s, c, i).wait_recv()
            total = total + got[s, c, i - 1].astype(f32)
        factor = lax.rsqrt(jnp.sum(total[rb:], axis=0, keepdims=True) / feats + 1e-05)
        red[s, mz, c] = (total[0:rb] * factor).astype(bf16)
        for i in order:
            gather(s, c, i, mz).start()

    def expand(s, cs):
        for c in cs:
            for i in order:
                gather(s, c, i, lax.rem(mz + nz - i, nz)).wait_recv()
        lhs = jnp.concatenate([jnp.concatenate([red[s, p, c].T for p in range(nz)], axis=1) for c in cs], axis=0)
        tile = out_ref.shape[2] // OUT_TILES
        for n in range(OUT_TILES):
            cols = slice(n * tile, (n + 1) * tile)
            out_ref[s, cs[0] * HD:(cs[-1] + 1) * HD, cols] = nn(lhs, ro_v[:, cols]).astype(bf16)

    both = (0, 1)
    heads(ST, [lambda i, j: (attend(0, i, j), local(1, i, j)), functools.partial(divide, 0, both)])
    project(0, both)
    heads(ST, [functools.partial(attend_half, 1, 0), functools.partial(divide, 1, (0,))])
    project(1, (0,))
    heads(ST, [functools.partial(attend_half, 1, 1), functools.partial(divide, 1, (1,))],
          hook=(2, lambda: (reduce(0, 0), reduce(0, 1))))
    project(1, (1,))
    loads[7].wait()
    reduce(1, 0)
    expand(0, both)
    reduce(1, 1)
    expand(1, (0,))
    expand(1, (1,))
    arrivals(send_e, recv_e, s1, r1).wait_send()
    arrivals(send_p, recv_p, s2, r2).wait_send()
    for s in range(SEQS):
        for c in both:
            for i in order:
                scatter(s, c, i).wait_send()
                gather(s, c, i, mz).wait_send()


def attention(nc, nz, q, k, v, qm, km, gain, ri, ro):
    hl, kvl, rank = qm.shape[0], km.shape[0], ri.shape[1]
    rows = SEQS * kvl * HD // nc
    rb = rank // nz
    states = SEQS * kvl
    st = min(ST, hl)
    vm, dma = pltpu.VMEM, pltpu.SemaphoreType.DMA
    hbm = pl.BlockSpec(memory_space=pltpu.HBM)
    vmem = pl.BlockSpec(memory_space=pltpu.VMEM)
    return pl.pallas_call(
        functools.partial(kernel, nc, nz, float(nz * hl * HD)),
        out_shape=pltpu.VMEM(q.shape, bf16),
        in_specs=[hbm, hbm, hbm, hbm, hbm, vmem, hbm, hbm],
        out_specs=pl.BlockSpec(memory_space=pltpu.VMEM),
        scratch_shapes=[
            vm(q.shape, bf16), vm(k.shape, bf16), vm(v.shape, bf16), vm(qm.shape, bf16),
            vm(km.shape, bf16), vm(ri.shape, bf16), vm(ro.shape, bf16),
            vm((rank, hl * HD), bf16), vm((hl, HD, HD), f32), vm((hl, HD), f32),
            vm((states, BLK, 2 * HD), bf16), vm((states, HD + 16, BLK), bf16), vm((states, HD + 16, 2 * HD), bf16),
            vm((SEQS, 2, hl * HD, HD), bf16), vm((SEQS, 16, BLK), f32), vm((SEQS, rb + 16, BLK), f32),
            vm((nc, rows, 3 * HD), bf16), vm((nc, rows, 3 * HD), bf16),
            vm((nc, rows, 3 * HD), bf16), vm((nc, rows, 3 * HD), bf16),
            vm((SEQS, 2, nz - 1, rb + 16, HD), bf16), vm((SEQS, 2, nz - 1, rb + 16, HD), bf16),
            vm((SEQS, nz, 2, rb, HD), bf16), vm((HD, HD), bf16),
            vm((st, HD, BLK), f32), vm((st, HD + 16, BLK), f32),
            dma((8,)), dma, dma, dma, dma,
            dma((2 * SEQS, nz)), dma((2 * SEQS, nz)), dma((2 * SEQS, nz)), dma((2 * SEQS, nz)),
        ] + [vm((SEQS * hl // st, 2, 2 * HD, HD), bf16)] * st + [
            vm((SEQS * hl // st, 2, BLK, HD), bf16)] * st + [vm((hl // st, HD + 16, BLK), f32)] * st,
        compiler_params=pltpu.CompilerParams(
            collective_id=0, has_side_effects=True, vmem_limit_bytes=VLIM * 2**20),
        name="attention",
    )(q, k, v, qm, km, gain, ri, ro)


def solution(mesh):
    nc, nz = mesh.shape["ctx"], mesh.shape["head"]

    def shards(queries, key_input, values, query_map, key_map, out_gain, rank_in, rank_out):
        return attention(nc, nz, queries, key_input, values, query_map, key_map,
                         out_gain.reshape(-1, HD), rank_in, rank_out)

    in_specs = (
        P(None, "ctx", "head"),
        P(None, "ctx", "head"),
        P(None, "ctx", "head"),
        P("head", None, None),
        P("head", None, None),
        P("head"),
        P("head", None),
        P(None, "head"),
    )
    out_specs = P(None, "ctx", "head")
    return jax.shard_map(shards, mesh=mesh, in_specs=in_specs, out_specs=out_specs, check_vma=False)
```

```python
import functools

import jax
import jax.numpy as jnp
from jax import lax
from jax.experimental import pallas as pl
from jax.experimental.pallas import tpu as pltpu
from jax.sharding import PartitionSpec as P

HD = 128
BLK = 256
SEQS = 2
ST = 8
VLIM = 59
OUT_TILES = 4
LOG2E = 1.4426950408889634
MESH = pl.DeviceIdType.MESH
bf16, f32 = jnp.bfloat16, jnp.float32


def nn(a, b):
    return jnp.dot(a, b, preferred_element_type=f32)


def tt(a, b):
    return lax.dot_general(a, b, (((0,), (1,)), ((), ())), preferred_element_type=f32)


def exps(scaled):
    pos = jnp.exp2(scaled - jnp.max(scaled, axis=0, keepdims=True))
    neg = jnp.exp2(jnp.min(scaled, axis=0, keepdims=True) - scaled)
    return pos, neg, jnp.sum(pos, axis=0, keepdims=True), jnp.sum(neg, axis=0, keepdims=True)


def kernel(nc, nz, feats, q_hbm, k_hbm, v_hbm, qm_hbm, km_hbm, gain_ref, ri_hbm, ro_hbm, out_ref,
           q_v, k_v, v_v, qm_v, km_v, ri_v, ro_v, rit, gcol, gains, fk, vta, pta, att, ssq, part,
           send_e, recv_e, send_p, recv_p, msg, got, red,
           tri, raw, tot, send_k, recv_k, sk, rk, in_sem, s1, r1, s2, r2, s3, r3, s4, r4, *per_head):
    n = len(per_head) // 3
    fq, wb, loc = per_head[:n], per_head[n:2 * n], per_head[2 * n:]
    hl, kvl = qm_v.shape[0], km_v.shape[0]
    groups = hl // kvl
    rank = ri_v.shape[1]
    rb = rank // nz
    rows = send_e.shape[1]
    per = HD // rows
    mc, mz = lax.axis_index("ctx"), lax.axis_index("head")

    loads = [(k_hbm, k_v), (v_hbm, v_v), (km_hbm, km_v), (qm_hbm, qm_v),
             (q_hbm.at[0], q_v.at[0]), (ri_hbm, ri_v), (q_hbm.at[1], q_v.at[1]), (ro_hbm, ro_v)]
    loads = [pltpu.make_async_copy(a, b, in_sem.at[i]) for i, (a, b) in enumerate(loads)]
    for load in loads:
        load.start()

    gains[...] = gain_ref[...].astype(f32)
    barrier = pltpu.get_barrier_semaphore()

    def greet_ctx(i, _):
        pl.semaphore_signal(barrier, inc=1, device_id=(lax.rem(mc + i, nc), mz), device_id_type=MESH)
        return 0

    lax.fori_loop(1, nc, greet_ctx, 0)
    for i in range(1, nz):
        pl.semaphore_signal(barrier, inc=1, device_id=(mc, lax.rem(mz + i, nz)), device_id_type=MESH)

    for load in loads[:3]:
        load.wait()
    for s in range(SEQS):
        for g in range(kvl):
            i = s * kvl + g
            lanes = slice(g * HD, (g + 1) * HD)
            pos, neg, zp, zn = exps(tt(km_v[g], k_v[s, :, lanes]) * LOG2E)
            feat = jnp.concatenate([pos * (1.0 / zp), neg * (1.0 / zn)], axis=0).astype(bf16)
            fk[i] = feat.T
            vta[i, 0:HD, :] = v_v[s, :, lanes].T
            vta[i, HD:HD + 16, :] = jnp.ones((16, BLK), bf16)
            state = nn(vta[i], fk[i])
            for p in range(per):
                j = i * per + p
                send_e[j] = state[p * rows:(p + 1) * rows].astype(bf16)
            send_k[2 * i:2 * i + 1, :] = state[HD:HD + 1, 0:HD]
            send_k[2 * i + 1:2 * i + 2, :] = state[HD:HD + 1, HD:]

    pl.semaphore_wait(barrier, nc - 1 + nz - 1)

    def exchange(src, dst, ssem, rsem, i):
        to = lax.rem(mc + i, nc)
        return pltpu.make_async_remote_copy(
            src_ref=src.at[to], dst_ref=dst.at[mc], send_sem=ssem, recv_sem=rsem,
            device_id=(to, mz), device_id_type=MESH)

    def arrivals(src, dst, ssem, rsem):
        return pltpu.make_async_remote_copy(
            src_ref=src.at[pl.ds(0, nc - 1)], dst_ref=dst.at[pl.ds(0, nc - 1)], send_sem=ssem, recv_sem=rsem,
            device_id=(lax.rem(mc + 1, nc), mz), device_id_type=MESH)

    for i in range(1, nc):
        exchange(send_e, recv_e, s1, r1, i).start()
    for i in range(1, nc):
        to = lax.rem(mc + i, nc)
        pltpu.make_async_remote_copy(
            src_ref=send_k, dst_ref=recv_k.at[mc], send_sem=sk, recv_sem=rk,
            device_id=(to, mz), device_id_type=MESH).start()
    recv_e[mc] = send_e[mc]
    recv_k[mc] = send_k[...]

    for load in loads[3:6]:
        load.wait()

    tri[...] = (lax.broadcasted_iota(jnp.int32, (HD, HD), 0)
                <= lax.broadcasted_iota(jnp.int32, (HD, HD), 1)).astype(f32).astype(bf16)

    ST = raw.shape[0]

    def joined(ref, i):
        return jnp.concatenate([ref[i, 0], ref[i, 1]], axis=1)

    def lanes_of(h):
        return pl.ds(pl.multiple_of(h * HD, HD), HD)

    def dots(s, i, j):
        h = i * ST + j
        raw[j] = tt(qm_v[h], q_v[s, :, lanes_of(h)]) * LOG2E

    def features(s, i, j):
        at = s * (hl // ST) + i
        for c in range(BLK // HD):
            pos, neg, zp, zn = exps(raw[j, :, c * HD:(c + 1) * HD])
            fq[j][at, c, 0:HD, :] = pos.astype(bf16)
            fq[j][at, c, HD:, :] = (neg * (zp / zn)).astype(bf16)

    def weigh(s, i, j):
        at = s * (hl // ST) + i
        score = nn(fk[s * kvl + (i * ST + j) // groups], joined(fq[j], at))
        wb[j][at, 0, 0:HD, :] = score[0:HD, 0:HD].astype(bf16) * tri[...]
        wb[j][at, 1, 0:HD, :] = score[0:HD, HD:].astype(bf16)
        wb[j][at, 0, HD:, :] = jnp.zeros((HD, HD), bf16)
        wb[j][at, 1, HD:, :] = score[HD:, HD:].astype(bf16) * tri[...]

    def prepare(i, j):
        at = lanes_of(i * ST + j)
        gcol[i * ST + j] = jnp.broadcast_to(gains[pl.ds(i * ST + j, 1), :], (HD, HD)).T
        rit[:, at] = ri_v[at, :].T

    def local(s, i, j):
        loc[j][i] = nn(vta[s * kvl + (i * ST + j) // groups], joined(wb[j], s * (hl // ST) + i))

    def attend(s, i, j):
        tot[j] = loc[j][i] + nn(pta[s * kvl + (i * ST + j) // groups], joined(fq[j], s * (hl // ST) + i))

    def attend_half(s, c, i, j):
        lanes = slice(c * HD, (c + 1) * HD)
        tot[j, :, lanes] = loc[j][i, :, lanes] + nn(
            pta[s * kvl + (i * ST + j) // groups], fq[j][s * (hl // ST) + i, c])

    def divide(s, cs, i, j):
        h = i * ST + j
        scale = gcol[h]
        for c in cs:
            lanes = slice(c * HD, (c + 1) * HD)
            out = tot[j, 0:HD, lanes] * (1.0 / tot[j, HD:HD + 1, lanes])
            ssq[s, :, lanes] += jnp.sum((out * out).reshape(HD // 16, 16, HD), axis=0)
            att[s, c, lanes_of(h), :] = (out * scale).astype(bf16)

    def heads(step, stages, hook=None):
        last, count = len(stages) - 1, hl // step

        def trip(i, live):
            for j in range(step):
                for k in range(last, -1, -1):
                    if k in live:
                        stages[k](i - k, j)

        def run(i, _):
            trip(i, range(last + 1))
            return 0

        for i in range(last):
            trip(i, range(0, i + 1))
        if hook is None:
            lax.fori_loop(last, count, run, 0)
        else:
            lax.fori_loop(last, hook[0], run, 0)
            hook[1]()
            lax.fori_loop(hook[0], count, run, 0)
        for i in range(count, count + last):
            trip(i, range(i - count + 1, last + 1))

    heads(ST, [lambda i, j: dots(0, i, j), lambda i, j: (features(0, i, j), prepare(i, j)),
               lambda i, j: weigh(0, i, j)])
    loads[6].wait()

    arrivals(send_e, recv_e, s1, r1).wait_recv()

    def scan(i, total):
        send_p[i] = total.astype(bf16)
        return total + recv_e[i].astype(f32)

    lax.fori_loop(0, nc, scan, jnp.zeros(send_p.shape[1:], f32))

    for i in range(1, nc):
        exchange(send_p, recv_p, s2, r2, i).start()
    recv_p[mc] = send_p[mc]

    heads(ST, [lambda i, j: (dots(1, i, j), local(0, i, j)), functools.partial(features, 1),
               functools.partial(weigh, 1)])

    arrivals(recv_k, recv_k, sk, rk).wait_recv()
    sums = lax.fori_loop(0, mc, lambda i, total: total + recv_k[i], jnp.zeros(send_k.shape, f32))
    arrivals(send_p, recv_p, s2, r2).wait_recv()
    for i in range(SEQS * kvl):
        for p in range(per):
            pta[i, p * rows:(p + 1) * rows, :] = recv_p[i * per + p]
        pta[i, HD:HD + 16, :] = jnp.broadcast_to(
            jnp.concatenate([sums[2 * i:2 * i + 1], sums[2 * i + 1:2 * i + 2]], axis=1), (16, BLK)).astype(bf16)

    ssq[...] = jnp.zeros_like(ssq)

    def scatter(s, c, i):
        to = lax.rem(mz + i, nz)
        return pltpu.make_async_remote_copy(
            src_ref=msg.at[s, c, i - 1], dst_ref=got.at[s, c, i - 1], send_sem=s3.at[2 * s + c, i],
            recv_sem=r3.at[2 * s + c, i], device_id=(mc, to), device_id_type=MESH)

    def gather(s, c, i, at):
        to = lax.rem(mz + i, nz)
        return pltpu.make_async_remote_copy(
            src_ref=red.at[s, at, c], dst_ref=red.at[s, at, c], send_sem=s4.at[2 * s + c, i],
            recv_sem=r4.at[2 * s + c, i], device_id=(mc, to), device_id_type=MESH)

    order = (2, 1, 3)
    half = (slice(0, HD), slice(HD, BLK))

    def project(s, cs):
        rhs = jnp.concatenate([att[s, c] for c in cs], axis=1)
        for i in order + (0,):
            to = lax.rem(mz + i, nz)
            block = nn(rit[pl.ds(pl.multiple_of(to * rb, rb), rb), :], rhs)
            for n, c in enumerate(cs):
                piece = jnp.concatenate([block[:, n * HD:(n + 1) * HD], ssq[s, :, half[c]]], axis=0)
                if i == 0:
                    part[s, :, half[c]] = piece
                else:
                    msg[s, c, i - 1] = piece.astype(bf16)
                    scatter(s, c, i).start()

    def reduce(s, c):
        total = part[s, :, half[c]]
        for i in order:
            scatter(s, c, i).wait_recv()
            total = total + got[s, c, i - 1].astype(f32)
        factor = lax.rsqrt(jnp.sum(total[rb:], axis=0, keepdims=True) / feats + 1e-05)
        red[s, mz, c] = (total[0:rb] * factor).astype(bf16)
        for i in order:
            gather(s, c, i, mz).start()

    def expand(s, cs):
        for c in cs:
            for i in order:
                gather(s, c, i, lax.rem(mz + nz - i, nz)).wait_recv()
        lhs = jnp.concatenate([jnp.concatenate([red[s, p, c].T for p in range(nz)], axis=1) for c in cs], axis=0)
        tile = out_ref.shape[2] // OUT_TILES
        for n in range(OUT_TILES):
            cols = slice(n * tile, (n + 1) * tile)
            out_ref[s, cs[0] * HD:(cs[-1] + 1) * HD, cols] = nn(lhs, ro_v[:, cols]).astype(bf16)

    both = (0, 1)
    heads(ST, [lambda i, j: (attend(0, i, j), local(1, i, j)), functools.partial(divide, 0, both)])
    project(0, both)
    heads(ST, [functools.partial(attend_half, 1, 0), functools.partial(divide, 1, (0,))])
    project(1, (0,))
    heads(ST, [functools.partial(attend_half, 1, 1), functools.partial(divide, 1, (1,))],
          hook=(2, lambda: (reduce(0, 0), reduce(0, 1))))
    project(1, (1,))
    loads[7].wait()
    reduce(1, 0)
    expand(0, both)
    reduce(1, 1)
    expand(1, (0,))
    expand(1, (1,))
    arrivals(send_e, recv_e, s1, r1).wait_send()
    arrivals(send_p, recv_p, s2, r2).wait_send()
    arrivals(recv_k, recv_k, sk, rk).wait_send()
    for s in range(SEQS):
        for c in both:
            for i in order:
                scatter(s, c, i).wait_send()
                gather(s, c, i, mz).wait_send()


def attention(nc, nz, q, k, v, qm, km, gain, ri, ro):
    hl, kvl, rank = qm.shape[0], km.shape[0], ri.shape[1]
    rows = SEQS * kvl * HD // nc
    rb = rank // nz
    states = SEQS * kvl
    st = min(ST, hl)
    vm, dma = pltpu.VMEM, pltpu.SemaphoreType.DMA
    hbm = pl.BlockSpec(memory_space=pltpu.HBM)
    vmem = pl.BlockSpec(memory_space=pltpu.VMEM)
    return pl.pallas_call(
        functools.partial(kernel, nc, nz, float(nz * hl * HD)),
        out_shape=pltpu.VMEM(q.shape, bf16),
        in_specs=[hbm, hbm, hbm, hbm, hbm, vmem, hbm, hbm],
        out_specs=pl.BlockSpec(memory_space=pltpu.VMEM),
        scratch_shapes=[
            vm(q.shape, bf16), vm(k.shape, bf16), vm(v.shape, bf16), vm(qm.shape, bf16),
            vm(km.shape, bf16), vm(ri.shape, bf16), vm(ro.shape, bf16),
            vm((rank, hl * HD), bf16), vm((hl, HD, HD), f32), vm((hl, HD), f32),
            vm((states, BLK, 2 * HD), bf16), vm((states, HD + 16, BLK), bf16), vm((states, HD + 16, 2 * HD), bf16),
            vm((SEQS, 2, hl * HD, HD), bf16), vm((SEQS, 16, BLK), f32), vm((SEQS, rb + 16, BLK), f32),
            vm((nc, rows, 2 * HD), bf16), vm((nc, rows, 2 * HD), bf16),
            vm((nc, rows, 2 * HD), bf16), vm((nc, rows, 2 * HD), bf16),
            vm((SEQS, 2, nz - 1, rb + 16, HD), bf16), vm((SEQS, 2, nz - 1, rb + 16, HD), bf16),
            vm((SEQS, nz, 2, rb, HD), bf16), vm((HD, HD), bf16),
            vm((st, HD, BLK), f32), vm((st, HD + 16, BLK), f32),
            vm((2 * states, HD), f32), vm((nc, 2 * states, HD), f32), dma, dma,
            dma((8,)), dma, dma, dma, dma,
            dma((2 * SEQS, nz)), dma((2 * SEQS, nz)), dma((2 * SEQS, nz)), dma((2 * SEQS, nz)),
        ] + [vm((SEQS * hl // st, 2, 2 * HD, HD), bf16)] * st + [
            vm((SEQS * hl // st, 2, BLK, HD), bf16)] * st + [vm((hl // st, HD + 16, BLK), f32)] * st,
        compiler_params=pltpu.CompilerParams(
            collective_id=0, has_side_effects=True, vmem_limit_bytes=VLIM * 2**20),
        name="attention",
    )(q, k, v, qm, km, gain, ri, ro)


def solution(mesh):
    nc, nz = mesh.shape["ctx"], mesh.shape["head"]

    def shards(queries, key_input, values, query_map, key_map, out_gain, rank_in, rank_out):
        return attention(nc, nz, queries, key_input, values, query_map, key_map,
                         out_gain.reshape(-1, HD), rank_in, rank_out)

    in_specs = (
        P(None, "ctx", "head"),
        P(None, "ctx", "head"),
        P(None, "ctx", "head"),
        P("head", None, None),
        P("head", None, None),
        P("head"),
        P("head", None),
        P(None, "head"),
    )
    out_specs = P(None, "ctx", "head")
    return jax.shard_map(shards, mesh=mesh, in_specs=in_specs, out_specs=out_specs, check_vma=False)
```

```python
import functools

import jax
import jax.numpy as jnp
from jax import lax
from jax.experimental import pallas as pl
from jax.experimental.pallas import tpu as pltpu
from jax.sharding import PartitionSpec as P

HD = 128
BLK = 256
SEQS = 2
ST = 8
VLIM = 59
OUT_TILES = 4
LOG2E = 1.4426950408889634
MESH = pl.DeviceIdType.MESH
bf16, f32 = jnp.bfloat16, jnp.float32


def nn(a, b):
    return jnp.dot(a, b, preferred_element_type=f32)


def tt(a, b):
    return lax.dot_general(a, b, (((0,), (1,)), ((), ())), preferred_element_type=f32)


def exps(scaled):
    pos = jnp.exp2(scaled - jnp.max(scaled, axis=0, keepdims=True))
    neg = jnp.exp2(jnp.min(scaled, axis=0, keepdims=True) - scaled)
    return pos, neg, jnp.sum(pos, axis=0, keepdims=True), jnp.sum(neg, axis=0, keepdims=True)


def kernel(nc, nz, feats, q_hbm, k_hbm, v_hbm, qm_hbm, km_hbm, gain_ref, ri_hbm, ro_hbm, out_ref,
           q_v, k_v, v_v, qm_v, km_v, ri_v, ro_v, rit, gcol, gains, fk, vta, pta, att, ssq, part,
           send_e, recv_e, send_p, recv_p, msg, got, red,
           tri, raw, tot, send_k, recv_k, sk, rk, in_sem, s1, r1, s2, r2, s3, r3, s4, r4, *per_head):
    n = len(per_head) // 3
    fq, wb, loc = per_head[:n], per_head[n:2 * n], per_head[2 * n:]
    hl, kvl = qm_v.shape[0], km_v.shape[0]
    groups = hl // kvl
    rank = ri_v.shape[1]
    rb = rank // nz
    rows = send_e.shape[1]
    per = HD // rows
    mc, mz = lax.axis_index("ctx"), lax.axis_index("head")

    loads = [(k_hbm, k_v), (v_hbm, v_v), (km_hbm, km_v), (qm_hbm, qm_v),
             (q_hbm.at[0], q_v.at[0]), (ri_hbm, ri_v), (q_hbm.at[1], q_v.at[1]), (ro_hbm, ro_v)]
    loads = [pltpu.make_async_copy(a, b, in_sem.at[i]) for i, (a, b) in enumerate(loads)]
    for load in loads:
        load.start()

    gains[...] = gain_ref[...].astype(f32)
    barrier = pltpu.get_barrier_semaphore()

    def greet_ctx(i, _):
        pl.semaphore_signal(barrier, inc=1, device_id=(lax.rem(mc + i, nc), mz), device_id_type=MESH)
        return 0

    lax.fori_loop(1, nc, greet_ctx, 0)
    for i in range(1, nz):
        pl.semaphore_signal(barrier, inc=1, device_id=(mc, lax.rem(mz + i, nz)), device_id_type=MESH)

    for load in loads[:3]:
        load.wait()
    sums = []
    for s in range(SEQS):
        for g in range(kvl):
            i = s * kvl + g
            lanes = slice(g * HD, (g + 1) * HD)
            pos, neg, zp, zn = exps(tt(km_v[g], k_v[s, :, lanes]) * LOG2E)
            feat = jnp.concatenate([pos * (1.0 / zp), neg * (1.0 / zn)], axis=0).astype(bf16)
            fk[i] = feat.T
            vta[i, 0:HD, :] = v_v[s, :, lanes].T
            vta[i, HD:HD + 16, :] = jnp.ones((16, BLK), bf16)
            state = nn(vta[i], fk[i])
            for p in range(per):
                j = i * per + p
                send_e[j] = state[p * rows:(p + 1) * rows].astype(bf16)
            sums += [state[HD:HD + 1, 0:HD], state[HD:HD + 1, HD:]]
    send_k[...] = jnp.concatenate(sums, axis=0).astype(bf16)

    pl.semaphore_wait(barrier, nc - 1 + nz - 1)

    def exchange(src, dst, ssem, rsem, i):
        to = lax.rem(mc + i, nc)
        return pltpu.make_async_remote_copy(
            src_ref=src.at[to], dst_ref=dst.at[mc], send_sem=ssem, recv_sem=rsem,
            device_id=(to, mz), device_id_type=MESH)

    def arrivals(src, dst, ssem, rsem):
        return pltpu.make_async_remote_copy(
            src_ref=src.at[pl.ds(0, nc - 1)], dst_ref=dst.at[pl.ds(0, nc - 1)], send_sem=ssem, recv_sem=rsem,
            device_id=(lax.rem(mc + 1, nc), mz), device_id_type=MESH)

    for i in range(1, nc):
        exchange(send_e, recv_e, s1, r1, i).start()
    for i in range(1, nc):
        to = lax.rem(mc + i, nc)
        pltpu.make_async_remote_copy(
            src_ref=send_k, dst_ref=recv_k.at[mc], send_sem=sk, recv_sem=rk,
            device_id=(to, mz), device_id_type=MESH).start()
    recv_e[mc] = send_e[mc]
    recv_k[mc] = send_k[...]

    for load in loads[3:6]:
        load.wait()

    tri[...] = (lax.broadcasted_iota(jnp.int32, (HD, HD), 0)
                <= lax.broadcasted_iota(jnp.int32, (HD, HD), 1)).astype(f32).astype(bf16)

    ST = raw.shape[0]

    def joined(ref, i):
        return jnp.concatenate([ref[i, 0], ref[i, 1]], axis=1)

    def lanes_of(h):
        return pl.ds(pl.multiple_of(h * HD, HD), HD)

    def dots(s, i, j):
        h = i * ST + j
        raw[j] = tt(qm_v[h], q_v[s, :, lanes_of(h)]) * LOG2E

    def features(s, i, j):
        at = s * (hl // ST) + i
        for c in range(BLK // HD):
            pos, neg, zp, zn = exps(raw[j, :, c * HD:(c + 1) * HD])
            fq[j][at, c, 0:HD, :] = pos.astype(bf16)
            fq[j][at, c, HD:, :] = (neg * (zp / zn)).astype(bf16)

    def weigh(s, i, j):
        at = s * (hl // ST) + i
        score = nn(fk[s * kvl + (i * ST + j) // groups], joined(fq[j], at))
        wb[j][at, 0, 0:HD, :] = score[0:HD, 0:HD].astype(bf16) * tri[...]
        wb[j][at, 1, 0:HD, :] = score[0:HD, HD:].astype(bf16)
        wb[j][at, 0, HD:, :] = jnp.zeros((HD, HD), bf16)
        wb[j][at, 1, HD:, :] = score[HD:, HD:].astype(bf16) * tri[...]

    def prepare(i, j):
        at = lanes_of(i * ST + j)
        gcol[i * ST + j] = jnp.broadcast_to(gains[pl.ds(i * ST + j, 1), :], (HD, HD)).T
        rit[:, at] = ri_v[at, :].T

    def local(s, i, j):
        loc[j][i] = nn(vta[s * kvl + (i * ST + j) // groups], joined(wb[j], s * (hl // ST) + i))

    def attend(s, i, j):
        tot[j] = loc[j][i] + nn(pta[s * kvl + (i * ST + j) // groups], joined(fq[j], s * (hl // ST) + i))

    def attend_half(s, c, i, j):
        lanes = slice(c * HD, (c + 1) * HD)
        tot[j, :, lanes] = loc[j][i, :, lanes] + nn(
            pta[s * kvl + (i * ST + j) // groups], fq[j][s * (hl // ST) + i, c])

    def divide(s, cs, i, j):
        h = i * ST + j
        scale = gcol[h]
        for c in cs:
            lanes = slice(c * HD, (c + 1) * HD)
            out = tot[j, 0:HD, lanes] * (1.0 / tot[j, HD:HD + 1, lanes])
            ssq[s, :, lanes] += jnp.sum((out * out).reshape(HD // 16, 16, HD), axis=0)
            att[s, c, lanes_of(h), :] = (out * scale).astype(bf16)

    def heads(step, stages, hook=None):
        last, count = len(stages) - 1, hl // step

        def trip(i, live):
            for j in range(step):
                for k in range(last, -1, -1):
                    if k in live:
                        stages[k](i - k, j)

        def run(i, _):
            trip(i, range(last + 1))
            return 0

        for i in range(last):
            trip(i, range(0, i + 1))
        if hook is None:
            lax.fori_loop(last, count, run, 0)
        else:
            lax.fori_loop(last, hook[0], run, 0)
            hook[1]()
            lax.fori_loop(hook[0], count, run, 0)
        for i in range(count, count + last):
            trip(i, range(i - count + 1, last + 1))

    heads(ST, [lambda i, j: dots(0, i, j), lambda i, j: (features(0, i, j), prepare(i, j)),
               lambda i, j: weigh(0, i, j)])
    loads[6].wait()

    arrivals(send_e, recv_e, s1, r1).wait_recv()

    def scan(i, total):
        send_p[i] = total.astype(bf16)
        return total + recv_e[i].astype(f32)

    lax.fori_loop(0, nc, scan, jnp.zeros(send_p.shape[1:], f32))

    for i in range(1, nc):
        exchange(send_p, recv_p, s2, r2, i).start()
    recv_p[mc] = send_p[mc]

    heads(ST, [lambda i, j: (dots(1, i, j), local(0, i, j)), functools.partial(features, 1),
               functools.partial(weigh, 1)])

    arrivals(recv_k, recv_k, sk, rk).wait_recv()
    sums = lax.fori_loop(0, mc, lambda i, total: total + recv_k[i].astype(f32), jnp.zeros(send_k.shape, f32))
    arrivals(send_p, recv_p, s2, r2).wait_recv()
    for i in range(SEQS * kvl):
        for p in range(per):
            pta[i, p * rows:(p + 1) * rows, :] = recv_p[i * per + p]
        pta[i, HD:HD + 16, :] = jnp.broadcast_to(
            jnp.concatenate([sums[2 * i:2 * i + 1], sums[2 * i + 1:2 * i + 2]], axis=1), (16, BLK)).astype(bf16)

    ssq[...] = jnp.zeros_like(ssq)

    def scatter(s, c, i):
        to = lax.rem(mz + i, nz)
        return pltpu.make_async_remote_copy(
            src_ref=msg.at[s, c, i - 1], dst_ref=got.at[s, c, i - 1], send_sem=s3.at[2 * s + c, i],
            recv_sem=r3.at[2 * s + c, i], device_id=(mc, to), device_id_type=MESH)

    def gather(s, c, i, at):
        to = lax.rem(mz + i, nz)
        return pltpu.make_async_remote_copy(
            src_ref=red.at[s, at, c], dst_ref=red.at[s, at, c], send_sem=s4.at[2 * s + c, i],
            recv_sem=r4.at[2 * s + c, i], device_id=(mc, to), device_id_type=MESH)

    order = (2, 1, 3)
    half = (slice(0, HD), slice(HD, BLK))

    def project(s, cs):
        rhs = jnp.concatenate([att[s, c] for c in cs], axis=1)
        for i in order + (0,):
            to = lax.rem(mz + i, nz)
            block = nn(rit[pl.ds(pl.multiple_of(to * rb, rb), rb), :], rhs)
            for n, c in enumerate(cs):
                piece = jnp.concatenate([block[:, n * HD:(n + 1) * HD], ssq[s, :, half[c]]], axis=0)
                if i == 0:
                    part[s, :, half[c]] = piece
                else:
                    msg[s, c, i - 1] = piece.astype(bf16)
                    scatter(s, c, i).start()

    def reduce(s, c):
        total = part[s, :, half[c]]
        for i in order:
            scatter(s, c, i).wait_recv()
            total = total + got[s, c, i - 1].astype(f32)
        factor = lax.rsqrt(jnp.sum(total[rb:], axis=0, keepdims=True) / feats + 1e-05)
        red[s, mz, c] = (total[0:rb] * factor).astype(bf16)
        for i in order:
            gather(s, c, i, mz).start()

    def expand(s, cs):
        for c in cs:
            for i in order:
                gather(s, c, i, lax.rem(mz + nz - i, nz)).wait_recv()
        lhs = jnp.concatenate([jnp.concatenate([red[s, p, c].T for p in range(nz)], axis=1) for c in cs], axis=0)
        tile = out_ref.shape[2] // OUT_TILES
        for n in range(OUT_TILES):
            cols = slice(n * tile, (n + 1) * tile)
            out_ref[s, cs[0] * HD:(cs[-1] + 1) * HD, cols] = nn(lhs, ro_v[:, cols]).astype(bf16)

    both = (0, 1)
    heads(ST, [lambda i, j: (attend(0, i, j), local(1, i, j)), functools.partial(divide, 0, both)])
    project(0, both)
    heads(ST, [functools.partial(attend_half, 1, 0), functools.partial(divide, 1, (0,))])
    project(1, (0,))
    heads(ST, [functools.partial(attend_half, 1, 1), functools.partial(divide, 1, (1,))],
          hook=(2, lambda: (reduce(0, 0), reduce(0, 1))))
    project(1, (1,))
    loads[7].wait()
    reduce(1, 0)
    expand(0, both)
    reduce(1, 1)
    expand(1, (0,))
    expand(1, (1,))
    arrivals(send_e, recv_e, s1, r1).wait_send()
    arrivals(send_p, recv_p, s2, r2).wait_send()
    arrivals(recv_k, recv_k, sk, rk).wait_send()
    for s in range(SEQS):
        for c in both:
            for i in order:
                scatter(s, c, i).wait_send()
                gather(s, c, i, mz).wait_send()


def attention(nc, nz, q, k, v, qm, km, gain, ri, ro):
    hl, kvl, rank = qm.shape[0], km.shape[0], ri.shape[1]
    rows = SEQS * kvl * HD // nc
    rb = rank // nz
    states = SEQS * kvl
    st = min(ST, hl)
    vm, dma = pltpu.VMEM, pltpu.SemaphoreType.DMA
    hbm = pl.BlockSpec(memory_space=pltpu.HBM)
    vmem = pl.BlockSpec(memory_space=pltpu.VMEM)
    return pl.pallas_call(
        functools.partial(kernel, nc, nz, float(nz * hl * HD)),
        out_shape=pltpu.VMEM(q.shape, bf16),
        in_specs=[hbm, hbm, hbm, hbm, hbm, vmem, hbm, hbm],
        out_specs=pl.BlockSpec(memory_space=pltpu.VMEM),
        scratch_shapes=[
            vm(q.shape, bf16), vm(k.shape, bf16), vm(v.shape, bf16), vm(qm.shape, bf16),
            vm(km.shape, bf16), vm(ri.shape, bf16), vm(ro.shape, bf16),
            vm((rank, hl * HD), bf16), vm((hl, HD, HD), f32), vm((hl, HD), f32),
            vm((states, BLK, 2 * HD), bf16), vm((states, HD + 16, BLK), bf16), vm((states, HD + 16, 2 * HD), bf16),
            vm((SEQS, 2, hl * HD, HD), bf16), vm((SEQS, 16, BLK), f32), vm((SEQS, rb + 16, BLK), f32),
            vm((nc, rows, 2 * HD), bf16), vm((nc, rows, 2 * HD), bf16),
            vm((nc, rows, 2 * HD), bf16), vm((nc, rows, 2 * HD), bf16),
            vm((SEQS, 2, nz - 1, rb + 16, HD), bf16), vm((SEQS, 2, nz - 1, rb + 16, HD), bf16),
            vm((SEQS, nz, 2, rb, HD), bf16), vm((HD, HD), bf16),
            vm((st, HD, BLK), f32), vm((st, HD + 16, BLK), f32),
            vm((2 * states, HD), bf16), vm((nc, 2 * states, HD), bf16), dma, dma,
            dma((8,)), dma, dma, dma, dma,
            dma((2 * SEQS, nz)), dma((2 * SEQS, nz)), dma((2 * SEQS, nz)), dma((2 * SEQS, nz)),
        ] + [vm((SEQS * hl // st, 2, 2 * HD, HD), bf16)] * st + [
            vm((SEQS * hl // st, 2, BLK, HD), bf16)] * st + [vm((hl // st, HD + 16, BLK), f32)] * st,
        compiler_params=pltpu.CompilerParams(
            collective_id=0, has_side_effects=True, vmem_limit_bytes=VLIM * 2**20),
        name="attention",
    )(q, k, v, qm, km, gain, ri, ro)


def solution(mesh):
    nc, nz = mesh.shape["ctx"], mesh.shape["head"]

    def shards(queries, key_input, values, query_map, key_map, out_gain, rank_in, rank_out):
        return attention(nc, nz, queries, key_input, values, query_map, key_map,
                         out_gain.reshape(-1, HD), rank_in, rank_out)

    in_specs = (
        P(None, "ctx", "head"),
        P(None, "ctx", "head"),
        P(None, "ctx", "head"),
        P("head", None, None),
        P("head", None, None),
        P("head"),
        P("head", None),
        P(None, "head"),
    )
    out_specs = P(None, "ctx", "head")
    return jax.shard_map(shards, mesh=mesh, in_specs=in_specs, out_specs=out_specs, check_vma=False)
```
